32 devices in a mesh: fsdp: 8 (over z, y), tp: 4 (over x, core).
Axes of the slice: x: 2, y: 2, z: 4, core: 2. Of those that a mesh axis runs over, the one named last changes fastest.
Arguments:
- hidden_in: bfloat16 [32768, 1024], P(('fsdp', 'tp')), may hold values from -8 to 8
- cotangent: bfloat16 [32768, 1024], P(('fsdp', 'tp')), may hold values from -6 to 6
- norm1_gain: bfloat16 [1024], replicated, may hold values from 0.5 to 1.5
- norm1_bias: bfloat16 [1024], replicated, may hold values from -3 to 3
- w_query: bfloat16 [1024, 1024], P('fsdp', 'tp'), may hold values from -0.25 to 0.25
- w_key: bfloat16 [1024, 1024], P('fsdp', 'tp'), may hold values from -0.1875 to 0.1875
- w_value: bfloat16 [1024, 1024], P('fsdp', 'tp'), may hold values from -0.1875 to 0.1875
- w_out: bfloat16 [1024, 1024], P('tp', 'fsdp'), may hold values from -1.5 to 1.5
- norm2_gain: bfloat16 [1024], replicated, may hold values from 0.5 to 1.5
- norm2_bias: bfloat16 [1024], replicated, may hold values from -3 to 3
- w_fc1: bfloat16 [1024, 4096], P('fsdp', 'tp'), may hold values from -0.1875 to 0.1875
- bias_fc1: bfloat16 [4096], P('tp'), may hold values from -3 to 3
- w_fc2: bfloat16 [4096, 1024], P('tp', 'fsdp'), may hold values from -0.09375 to 0.09375
- bias_fc2: bfloat16 [1024], replicated, may hold values from -3 to 3
- segments: int32 [8, 4096], P('fsdp'), may hold values from 0 to 9, as said below
- random_blocks: int32 [8, 16, 62, 3], P('fsdp', 'tp'), may hold values from 1 to 62, as said below
Outputs:
- layer_out: bfloat16 [32768, 1024], P(('fsdp', 'tp'))
- grad_input: float32 [32768, 1024], P(('fsdp', 'tp'))
- grad_norm1_gain: float32 [1024], replicated
- grad_norm1_bias: float32 [1024], replicated
- grad_w_query: float32 [1024, 1024], P('fsdp', 'tp')
- grad_w_key: float32 [1024, 1024], P('fsdp', 'tp')
- grad_w_value: float32 [1024, 1024], P('fsdp', 'tp')
- grad_w_out: float32 [1024, 1024], P('tp', 'fsdp')
- grad_norm2_gain: float32 [1024], replicated
- grad_norm2_bias: float32 [1024], replicated
- grad_w_fc1: float32 [1024, 4096], P('fsdp', 'tp')
- grad_bias_fc1: float32 [4096], P('tp')
- grad_w_fc2: float32 [4096, 1024], P('tp', 'fsdp')
- grad_bias_fc2: float32 [1024], replicated
- residual_rms: float32 [4], replicated
The draws below stay inside these ranges and needn't reach their ends.
Inputs may be any that keep to these rules, and one draw needn't show every extreme that they name: `segments`: in each row the segment numbers never fall over the non-padding tokens, all of 1 to 9 occur, and the row ends with 1 to 512 padding tokens of segment 0. `random_blocks`: for the query block b of row b - 1, the 3 numbers are distinct and none equals b - 1, b or b + 1.
All inputs are finite; a program needn't handle non-finite values.
Results may differ from the reference program's by a relative error of at most 0.012.
The reference program's roundings to bfloat16 on the way count: a program that leaves them out, or rounds other values in their place, can miss the bound.
Values may be sent and summed in bfloat16 or wider, within the bound.
No kernel may reach another device: no remote copies, remote signals or barrier semaphores. Data moves between devices by JAX's collectives and lax.ppermute only.
A program may use at most 448 MiB of HBM per device.

```python
import math
import jax
import jax.numpy as jnp
from jax import lax

D = 1024
HEADS = 16
HEAD_DIM = 64
FF = 4096
BLOCK = 64
RAND = 3
SEQ = 4096
NSEQ = 8
TOKENS = 32768
NBLK = 64


def draw_hidden_in(key, part):
    own_key = jax.random.fold_in(key, 5)
    where_row = jnp.arange(TOKENS, dtype=jnp.float32)[:, None] / (TOKENS - 1)
    values = jnp.clip(jax.random.normal(own_key, (TOKENS, D), jnp.float32), -4.0, 4.0)
    scale_row = 0.6 * jnp.exp(where_row * math.log(3.0))
    return (values * scale_row).astype(jnp.bfloat16)


def segment_row(row_key):
    usable = SEQ - SEQ // 8
    cut_key, pad_key = jax.random.split(row_key)
    cuts = jax.random.permutation(cut_key, usable - 1)[:8] + 1
    pad_count = jax.random.randint(pad_key, (), 1, SEQ // 8 + 1)
    positions = jnp.arange(SEQ, dtype=jnp.int32)
    seg_ids = 1 + jnp.sum((cuts[None, :] <= positions[:, None]).astype(jnp.int32), axis=1)
    return jnp.where(positions >= SEQ - pad_count, 0, seg_ids).astype(jnp.int32)


def draw_segments(key, part):
    row_keys = jax.random.split(jax.random.fold_in(key, 11), NSEQ)
    return jax.vmap(segment_row)(row_keys)


def pick_offsets(row_key):
    return jax.random.permutation(row_key, NBLK - 5)[:RAND]


def draw_random_blocks(key, part):
    row_keys = jax.random.split(jax.random.fold_in(key, 23), NSEQ * HEADS * (NBLK - 2))
    offsets = jax.vmap(pick_offsets)(row_keys).reshape(NSEQ, HEADS, NBLK - 2, RAND)
    query_blk = jnp.arange(1, NBLK - 1, dtype=jnp.int32)[None, None, :, None]
    picked = 1 + offsets.astype(jnp.int32)
    return jnp.where(picked >= query_blk - 1, picked + 3, picked).astype(jnp.int32)


def steps_of(key, shape, cuts, low, high):
    loudness = 1.0
    for dim, parts in cuts:
        heights = jax.random.uniform(jax.random.fold_in(jax.random.fold_in(key, 6), dim), (parts,), jnp.float32, low / len(cuts), high / len(cuts))
        loudness = loudness * jnp.repeat(jnp.exp(heights), shape[dim] // parts).reshape((-1,) + (1,) * (len(shape) - 1 - dim))
    return loudness


def scatter_about(stream_key, shape, spread, reach, pieces=(), held_as=jnp.bfloat16):
    loudness = steps_of(stream_key, shape, pieces, -0.22, 0.18) if pieces else 1.0
    drawn = jax.random.normal(stream_key, shape, jnp.float32) * spread * loudness
    return jnp.minimum(jnp.maximum(drawn, -reach), reach).astype(held_as)


def setup_inputs(seed: int = 0) -> dict:
    streams_of = jax.random.split(jax.random.key(seed), 17)
    hidden_in = draw_hidden_in(jax.random.fold_in(streams_of[16], 71), 0)
    cotangent = scatter_about(streams_of[1], (TOKENS, D), 1.0, 6.0, ((0, 32),))
    norm1_gain = jnp.clip(1.0 + 0.1 * jax.random.normal(streams_of[2], (D,), jnp.float32), 0.5, 1.5).astype(jnp.bfloat16)
    norm1_bias = scatter_about(streams_of[3], (D,), 0.3, 3.0)
    w_query = scatter_about(streams_of[4], (D, D), (D // 2) ** -0.5, 0.25, ((0, 8), (1, 4)))
    w_key = scatter_about(streams_of[5], (D, D), D ** -0.5, 0.1875, ((0, 8), (1, 4)))
    w_value = scatter_about(streams_of[6], (D, D), D ** -0.5, 0.1875, ((0, 8), (1, 4)))
    w_out = scatter_about(streams_of[7], (D, D), (D // 64) ** -0.5, 1.5, ((0, 4), (1, 8)))
    norm2_gain = jnp.clip(1.0 + 0.1 * jax.random.normal(streams_of[8], (D,), jnp.float32), 0.5, 1.5).astype(jnp.bfloat16)
    norm2_bias = scatter_about(streams_of[9], (D,), 0.3, 3.0)
    w_fc1 = scatter_about(streams_of[10], (D, FF), D ** -0.5, 0.1875, ((0, 8), (1, 4)))
    bias_fc1 = scatter_about(streams_of[11], (FF,), 0.5, 3.0, ((0, 4),))
    w_fc2 = scatter_about(streams_of[12], (FF, D), FF ** -0.5, 0.09375, ((0, 4), (1, 8)))
    bias_fc2 = scatter_about(streams_of[13], (D,), 0.3, 3.0)
    segments = draw_segments(jax.random.fold_in(streams_of[16], 71), 0)
    random_blocks = draw_random_blocks(jax.random.fold_in(streams_of[16], 71), 0)
    return dict(hidden_in=hidden_in, cotangent=cotangent, norm1_gain=norm1_gain, norm1_bias=norm1_bias, w_query=w_query, w_key=w_key, w_value=w_value, w_out=w_out, norm2_gain=norm2_gain, norm2_bias=norm2_bias, w_fc1=w_fc1, bias_fc1=bias_fc1, w_fc2=w_fc2, bias_fc2=bias_fc2, segments=segments, random_blocks=random_blocks)


@jax.custom_vjp
def low(v):
    return lax.optimization_barrier(v.astype(jnp.bfloat16)).astype(jnp.float32)

@jax.custom_vjp
def low_back(v):
    return v

def low_keep(v):
    return (low(v), None)

def low_pass(kept, grad):
    return (grad,)

def back_keep(v):
    return (v, None)

def back_low(kept, grad):
    return (low(grad),)
low.defvjp(low_keep, low_pass)
low_back.defvjp(back_keep, back_low)
highest = lax.Precision.HIGHEST
eps_norm = 1e-05
neg_large = -1e+30

def matmul(left, right):
    return jnp.dot(left, right, precision=highest, preferred_element_type=jnp.float32)

def layer_norm(source, gain_vec, shift_vec):
    average = lax.optimization_barrier(jnp.mean(source, axis=-1, keepdims=True))
    centred = source - average
    variance = lax.optimization_barrier(jnp.mean(centred * centred, axis=-1, keepdims=True))
    return centred * lax.rsqrt(variance + eps_norm) * gain_vec + shift_vec

def block_allowed(random_rows):
    query_blk = jnp.arange(NBLK, dtype=jnp.int32)[:, None]
    key_blk = jnp.arange(NBLK, dtype=jnp.int32)[None, :]
    border = (query_blk == 0) | (query_blk == NBLK - 1) | (key_blk == 0) | (key_blk == NBLK - 1)
    fixed = (jnp.abs(query_blk - key_blk) <= 1) | border
    filler = jnp.full((HEADS, 1, RAND), -1, jnp.int32)
    padded = jnp.concatenate([filler, random_rows.astype(jnp.int32), filler], 1)
    chosen = jnp.any(padded[:, :, :, None] == jnp.arange(NBLK, dtype=jnp.int32)[None, None, None, :], axis=2)
    return fixed[None, :, :] | chosen

def head_attend(head_items, token_ok):
    head_query, head_key, head_value, block_ok = head_items
    allowed = jnp.repeat(jnp.repeat(block_ok, BLOCK, axis=0), BLOCK, axis=1) & token_ok
    scores = low_back(matmul(head_query, head_key.T))
    scores = jnp.where(allowed, scores, neg_large)
    row_max = lax.optimization_barrier(jnp.max(scores, axis=1, keepdims=True))
    exponent = jnp.exp(scores - row_max)
    attn_probs = exponent / lax.optimization_barrier(jnp.sum(exponent, axis=1, keepdims=True))
    return matmul(low(attn_probs), head_value)

def split_heads(flat):
    return flat.reshape(SEQ, HEADS, HEAD_DIM).transpose(1, 0, 2)

def sequence_forward(weights, seq_rows, seq_segs, random_rows):
    gain_first, shift_first, w_q, w_k, w_v, w_o, gain_second, shift_second, w_up, bias_up, w_down, bias_down = weights
    normed_first = low(layer_norm(seq_rows, gain_first, shift_first))
    queries = low(low_back(matmul(normed_first, w_q) * HEAD_DIM ** (-0.5)))
    key_rows = low(low_back(matmul(normed_first, w_k)))
    value_rows = low(low_back(matmul(normed_first, w_v)))
    positions = jnp.arange(SEQ, dtype=jnp.int32)
    token_ok = (seq_segs[:, None] == seq_segs[None, :]) & (seq_segs[None, :] != 0) | (positions[:, None] == positions[None, :])
    attend_one = jax.checkpoint(head_attend)

    def per_head(head_items):
        return attend_one(head_items, token_ok)
    heads_out = lax.map(per_head, (split_heads(queries), split_heads(key_rows), split_heads(value_rows), block_allowed(random_rows)))
    context = low(low_back(heads_out.transpose(1, 0, 2).reshape(SEQ, D)))
    attn_branch = low_back(matmul(context, w_o))
    middle = seq_rows + attn_branch
    normed_second = low(layer_norm(middle, gain_second, shift_second))
    pre_act = low_back(matmul(normed_second, w_up) + bias_up)
    hidden_low = low(jax.nn.gelu(pre_act, approximate=True))
    ffn_branch = low_back(matmul(hidden_low, w_down) + bias_down)
    return (middle + ffn_branch, (seq_rows, attn_branch, middle, ffn_branch))

def reference(hidden_in, cotangent, norm1_gain, norm1_bias, w_query, w_key, w_value, w_out, norm2_gain, norm2_bias, w_fc1, bias_fc1, w_fc2, bias_fc2, segments, random_blocks):
    params = tuple((item.astype(jnp.float32) for item in (norm1_gain, norm1_bias, w_query, w_key, w_value, w_out, norm2_gain, norm2_bias, w_fc1, bias_fc1, w_fc2, bias_fc2)))
    rows_in = hidden_in.astype(jnp.float32)

    def forward(rows_all, weights):

        def one_sequence(running, seq_items):
            seq_rows, seq_segs, random_rows = seq_items
            seq_out, branches = sequence_forward(weights, seq_rows, seq_segs, random_rows)
            valid_rows = (seq_segs != 0).astype(jnp.float32)[:, None]
            square_sums = jnp.stack([jnp.sum(valid_rows * branch * branch) for branch in branches])
            return (running + square_sums, seq_out)
        square_sums, seq_outs = lax.scan(one_sequence, jnp.zeros((4,), jnp.float32), (rows_all.reshape(NSEQ, SEQ, D), segments, random_blocks))
        return (seq_outs.reshape(TOKENS, D), square_sums)
    result, pullback, square_sums = jax.vjp(forward, rows_in, params, has_aux=True)
    grad_rows, grad_params = pullback(cotangent.astype(jnp.float32))
    valid_count = jnp.sum((segments != 0).astype(jnp.float32))
    residual_rms = jnp.sqrt(square_sums / (valid_count * D))
    return (result.astype(jnp.bfloat16), grad_rows, grad_params[0], grad_params[1], grad_params[2], grad_params[3], grad_params[4], grad_params[5], grad_params[6], grad_params[7], grad_params[8], grad_params[9], grad_params[10], grad_params[11], residual_rms)
```

```python
from functools import partial
import jax, jax.numpy as jnp
from jax import lax
from jax.experimental import pallas as pl
from jax.experimental.pallas import tpu as pltpu
from jax.sharding import PartitionSpec as P

HEAD_DIM = 64
BLOCK = 64
LANES = 128
F32 = jnp.float32
LOW = jnp.bfloat16
neg_large = -1e30


def dot_nn(a, b):
    return lax.dot_general(a, b, (((1,), (0,)), ((), ())), preferred_element_type=F32)


def dot_nt(a, b):
    return lax.dot_general(a, b, (((1,), (1,)), ((), ())), preferred_element_type=F32)


def dot_tn(a, b):
    return lax.dot_general(a, b, (((0,), (0,)), ((), ())), preferred_element_type=F32)


class Walk:
    def __init__(self, rank_ref, pick_ref, heads, seq, rand):
        self.rank = rank_ref[0]
        self.pick_ref = pick_ref
        self.heads = heads
        self.rand = rand
        self.nblocks = seq // BLOCK

    def place(self, blk):
        per = self.nblocks // 4
        chunk = lax.bitwise_xor(lax.div(blk, per), self.rank)
        return pl.multiple_of((chunk * per + lax.rem(blk, per)) * BLOCK, BLOCK)

    def picked(self, blk, head, slot):
        return self.pick_ref[(head * (self.nblocks - 2) + blk - 1) * self.rand + slot]


def left_lanes(rows):
    return lax.broadcasted_iota(jnp.int32, (rows, LANES), 1) < HEAD_DIM


def spread_heads(rows, heads):
    tall = jnp.concatenate([rows.astype(F32)] * heads, axis=0)
    width = heads * HEAD_DIM
    row_head = lax.broadcasted_iota(jnp.int32, (heads * BLOCK, width), 0) // BLOCK
    col_head = lax.broadcasted_iota(jnp.int32, (heads * BLOCK, width), 1) // HEAD_DIM
    return jnp.where(row_head == col_head, tall, 0.0).astype(LOW)


def own_heads(full, heads):
    left = left_lanes(BLOCK)
    halves = []
    for pair in range(heads // 2):
        cols = slice(pair * LANES, (pair + 1) * LANES)
        first = full[2 * pair * BLOCK : (2 * pair + 1) * BLOCK, cols]
        second = full[(2 * pair + 1) * BLOCK : (2 * pair + 2) * BLOCK, cols]
        halves.append(jnp.where(left, first, second))
    return jnp.concatenate(halves, axis=1)


def gather_rows(ref, base, walk, blk):
    heads = walk.heads
    width = heads * HEAD_DIM
    left = left_lanes(BLOCK)
    parts = [
        ref[pl.ds(walk.place(at), BLOCK), base : base + width]
        for at in (blk - 1, blk, blk + 1, 0, walk.nblocks - 1)
    ]
    for slot in range(walk.rand):
        halves = []
        for pair in range(heads // 2):
            cols = slice(base + pair * LANES, base + (pair + 1) * LANES)
            first = ref[pl.ds(walk.place(walk.picked(blk, 2 * pair, slot)), BLOCK), cols]
            second = ref[pl.ds(walk.place(walk.picked(blk, 2 * pair + 1, slot)), BLOCK), cols]
            halves.append(jnp.where(left, first, second))
        parts.append(jnp.concatenate(halves, axis=1))
    return jnp.concatenate(parts, axis=0)


def key_marks(mark_ref, walk, blk):
    heads = walk.heads
    left = left_lanes(BLOCK)

    def rows_at(at):
        return mark_ref[pl.ds(pl.multiple_of(at * BLOCK, BLOCK), BLOCK), :]

    before = jnp.where(blk == 1, -1, rows_at(blk - 1))
    after = jnp.where(blk == walk.nblocks - 2, -1, rows_at(blk + 1))
    parts = [
        jnp.concatenate([rows] * (heads // 2), axis=1)
        for rows in (before, rows_at(blk), after, rows_at(0), rows_at(walk.nblocks - 1))
    ]
    for slot in range(walk.rand):
        halves = []
        for pair in range(heads // 2):
            first = rows_at(walk.picked(blk, 2 * pair, slot))
            second = rows_at(walk.picked(blk, 2 * pair + 1, slot))
            halves.append(jnp.where(left, first, second))
        parts.append(jnp.concatenate(halves, axis=1))
    return jnp.concatenate(parts, axis=0)


def chunk_marks(mark_ref, walk, at, size):
    per = walk.nblocks // 4 * BLOCK
    chunk = lax.bitwise_xor(lax.div(at, per), walk.rank)
    natural = pl.multiple_of(chunk * per + lax.rem(at, per), BLOCK)
    rows = mark_ref[pl.ds(natural, size), :]
    return jnp.concatenate([rows] * (walk.heads // 2), axis=1)


def forward_kernel(rank_ref, pick_ref, qkv_ref, mark_ref, qmark_ref, out_ref, score_ref, *, heads, rand, span):
    seq = qkv_ref.shape[0]
    width = heads * HEAD_DIM
    walk = Walk(rank_ref, pick_ref, heads, seq, rand)

    def middle(blk):
        query = spread_heads(qkv_ref[pl.ds(walk.place(blk), BLOCK), 0:width], heads)
        keys = gather_rows(qkv_ref, width, walk, blk)
        score = dot_nt(keys, query)
        ok = key_marks(mark_ref, walk, blk) == qmark_ref[pl.ds(blk, 1), :]
        score = jnp.where(ok, score, neg_large)
        expo = jnp.exp(score - jnp.max(score, axis=0, keepdims=True))
        probs = (expo * (1.0 / jnp.sum(expo, axis=0, keepdims=True))).astype(LOW)
        values = gather_rows(qkv_ref, 2 * width, walk, blk)
        out_ref[pl.ds(walk.place(blk), BLOCK), :] = own_heads(dot_tn(probs, values), heads).astype(LOW)

    def pair(step, carry):
        middle(2 * step + 1)
        middle(2 * step + 2)
        return carry

    lax.fori_loop(0, (walk.nblocks - 2) // 2, pair, 0)

    for blk in (0, walk.nblocks - 1):
        query = spread_heads(qkv_ref[pl.ds(walk.place(blk), BLOCK), 0:width], heads)
        qmark = qmark_ref[blk : blk + 1, :]

        def scores_at(step, top):
            at = pl.multiple_of(step * span, span)
            score = dot_nt(qkv_ref[pl.ds(at, span), width : 2 * width], query)
            score = jnp.where(chunk_marks(mark_ref, walk, at, span) == qmark, score, neg_large)
            score_ref[pl.ds(at, span), :] = score
            return jnp.maximum(top, jnp.max(score, axis=0, keepdims=True))

        def expo_at(step, total, top):
            at = pl.multiple_of(step * span, span)
            expo = jnp.exp(score_ref[pl.ds(at, span), :] - top)
            score_ref[pl.ds(at, span), :] = expo
            return total + jnp.sum(expo, axis=0, keepdims=True)

        def value_at(step, total, scale):
            at = pl.multiple_of(step * span, span)
            probs = (score_ref[pl.ds(at, span), :] * scale).astype(LOW)
            return total + dot_tn(probs, qkv_ref[pl.ds(at, span), 2 * width : 3 * width])

        top = jnp.full((1, heads * BLOCK), neg_large, F32)
        top = lax.fori_loop(0, seq // span, scores_at, top)
        total = lax.fori_loop(0, seq // span, partial(expo_at, top=top), jnp.zeros_like(top))
        full = lax.fori_loop(0, seq // span, partial(value_at, scale=1.0 / total), jnp.zeros((heads * BLOCK, width), F32))
        out_ref[pl.ds(walk.place(blk), BLOCK), :] = own_heads(full, heads).astype(LOW)


def backward_kernel(rank_ref, pick_ref, qkv_ref, grad_ref, mark_ref, qmark_ref, out_ref, key_acc, value_acc, score_ref, dprob_ref, *, heads, rand, span):
    seq = qkv_ref.shape[0]
    width = heads * HEAD_DIM
    walk = Walk(rank_ref, pick_ref, heads, seq, rand)
    left = left_lanes(BLOCK)

    def clear(step, carry):
        at = pl.multiple_of(step * span, span)
        key_acc[pl.ds(at, span), :] = jnp.zeros((span, width), F32)
        value_acc[pl.ds(at, span), :] = jnp.zeros((span, width), F32)
        return carry

    lax.fori_loop(0, seq // span, clear, 0)

    def add_rows(acc, rows, blk):
        for index, at in enumerate((blk - 1, blk, blk + 1, 0, walk.nblocks - 1)):
            acc[pl.ds(walk.place(at), BLOCK), :] += rows[index * BLOCK : (index + 1) * BLOCK, :]
        for slot in range(rand):
            row = (5 + slot) * BLOCK
            for pair in range(heads // 2):
                cols = slice(pair * LANES, (pair + 1) * LANES)
                piece = rows[row : row + BLOCK, cols]
                acc[pl.ds(walk.place(walk.picked(blk, 2 * pair, slot)), BLOCK), cols] += jnp.where(left, piece, 0.0)
                acc[pl.ds(walk.place(walk.picked(blk, 2 * pair + 1, slot)), BLOCK), cols] += jnp.where(left, 0.0, piece)

    def middle(blk):
        place = walk.place(blk)
        query = spread_heads(qkv_ref[pl.ds(place, BLOCK), 0:width], heads)
        grad = spread_heads(grad_ref[pl.ds(place, BLOCK), :], heads)
        keys = gather_rows(qkv_ref, width, walk, blk)
        values = gather_rows(qkv_ref, 2 * width, walk, blk)
        score = dot_nt(keys, query)
        ok = key_marks(mark_ref, walk, blk) == qmark_ref[pl.ds(blk, 1), :]
        score = jnp.where(ok, score, neg_large)
        expo = jnp.exp(score - jnp.max(score, axis=0, keepdims=True))
        probs = expo * (1.0 / jnp.sum(expo, axis=0, keepdims=True))
        dprob = dot_nt(values, grad)
        delta = jnp.sum(probs * dprob, axis=0, keepdims=True)
        dscore = (probs * (dprob - delta)).astype(LOW)
        dvalue = dot_nn(probs.astype(LOW), grad)
        dkey = dot_nn(dscore, query)
        dquery = own_heads(dot_tn(dscore, keys), heads)
        out_ref[pl.ds(place, BLOCK), 0:width] = dquery.astype(LOW)
        return dkey, dvalue

    def pair(step, carry):
        dkey_a, dvalue_a = middle(2 * step + 1)
        dkey_b, dvalue_b = middle(2 * step + 2)
        add_rows(key_acc, dkey_a, 2 * step + 1)
        add_rows(value_acc, dvalue_a, 2 * step + 1)
        add_rows(key_acc, dkey_b, 2 * step + 2)
        add_rows(value_acc, dvalue_b, 2 * step + 2)
        return carry

    lax.fori_loop(0, (walk.nblocks - 2) // 2, pair, 0)

    for blk in (0, walk.nblocks - 1):
        place = walk.place(blk)
        query = spread_heads(qkv_ref[pl.ds(place, BLOCK), 0:width], heads)
        grad = spread_heads(grad_ref[pl.ds(place, BLOCK), :], heads)
        qmark = qmark_ref[blk : blk + 1, :]

        def scores_at(step, top):
            at = pl.multiple_of(step * span, span)
            score = dot_nt(qkv_ref[pl.ds(at, span), width : 2 * width], query)
            score = jnp.where(chunk_marks(mark_ref, walk, at, span) == qmark, score, neg_large)
            score_ref[pl.ds(at, span), :] = score
            dprob_ref[pl.ds(at, span), :] = dot_nt(qkv_ref[pl.ds(at, span), 2 * width : 3 * width], grad)
            return jnp.maximum(top, jnp.max(score, axis=0, keepdims=True))

        def expo_at(step, carry, top):
            total, weighted = carry
            at = pl.multiple_of(step * span, span)
            expo = jnp.exp(score_ref[pl.ds(at, span), :] - top)
            score_ref[pl.ds(at, span), :] = expo
            return (
                total + jnp.sum(expo, axis=0, keepdims=True),
                weighted + jnp.sum(expo * dprob_ref[pl.ds(at, span), :], axis=0, keepdims=True),
            )

        def grads_at(step, dquery, scale, delta):
            at = pl.multiple_of(step * span, span)
            probs = score_ref[pl.ds(at, span), :] * scale
            dscore = (probs * (dprob_ref[pl.ds(at, span), :] - delta)).astype(LOW)
            value_acc[pl.ds(at, span), :] += dot_nn(probs.astype(LOW), grad)
            key_acc[pl.ds(at, span), :] += dot_nn(dscore, query)
            return dquery + dot_tn(dscore, qkv_ref[pl.ds(at, span), width : 2 * width])

        top = jnp.full((1, heads * BLOCK), neg_large, F32)
        top = lax.fori_loop(0, seq // span, scores_at, top)
        total, weighted = lax.fori_loop(0, seq // span, partial(expo_at, top=top), (jnp.zeros_like(top), jnp.zeros_like(top)))
        scale = 1.0 / total
        full = lax.fori_loop(0, seq // span, partial(grads_at, scale=scale, delta=weighted * scale), jnp.zeros((heads * BLOCK, width), F32))
        out_ref[pl.ds(place, BLOCK), 0:width] = own_heads(full, heads).astype(LOW)

    def finish(step, carry):
        at = pl.multiple_of(step * span, span)
        out_ref[pl.ds(at, span), width : 2 * width] = key_acc[pl.ds(at, span), :].astype(LOW)
        out_ref[pl.ds(at, span), 2 * width : 3 * width] = value_acc[pl.ds(at, span), :].astype(LOW)
        return carry

    lax.fori_loop(0, seq // span, finish, 0)


def token_marks(seq_segs, heads):
    seq = seq_segs.shape[0]
    marks = jnp.where(seq_segs != 0, seq_segs, 1000 + jnp.arange(seq, dtype=jnp.int32))
    by_row = jnp.broadcast_to(marks[:, None], (seq, LANES))
    by_block = jnp.tile(marks.reshape(seq // BLOCK, BLOCK), (1, heads))
    return by_row, by_block


SMEM_SPEC = pl.BlockSpec(memory_space=pltpu.SMEM)
VMEM_SPEC = pl.BlockSpec(memory_space=pltpu.VMEM)


def attend(rank, picks, qkv, marks):
    heads, _, rand = picks.shape
    seq = qkv.shape[0]
    width = heads * HEAD_DIM
    span = min(512, seq // 4)
    return pl.pallas_call(
        partial(forward_kernel, heads=heads, rand=rand, span=span),
        out_shape=jax.ShapeDtypeStruct((seq, width), LOW),
        in_specs=[SMEM_SPEC, SMEM_SPEC, VMEM_SPEC, VMEM_SPEC, VMEM_SPEC],
        out_specs=VMEM_SPEC,
        scratch_shapes=[pltpu.VMEM((seq, heads * BLOCK), F32)],
        name="attend",
    )(rank, picks.reshape(-1), qkv, *marks)


def attend_back(rank, picks, qkv, grad_context, marks):
    heads, _, rand = picks.shape
    seq = qkv.shape[0]
    width = heads * HEAD_DIM
    span = min(512, seq // 4)
    return pl.pallas_call(
        partial(backward_kernel, heads=heads, rand=rand, span=span),
        out_shape=jax.ShapeDtypeStruct((seq, 3 * width), LOW),
        in_specs=[SMEM_SPEC, SMEM_SPEC, VMEM_SPEC, VMEM_SPEC, VMEM_SPEC, VMEM_SPEC],
        out_specs=VMEM_SPEC,
        scratch_shapes=[pltpu.VMEM((seq, width), F32)] * 2 + [pltpu.VMEM((seq, heads * BLOCK), F32)] * 2,
        name="attend_back",
    )(rank, picks.reshape(-1), qkv, grad_context, *marks)


eps_norm = 1e-05


def norm_rows(source, gain_vec, shift_vec):
    average = jnp.mean(source, axis=-1, keepdims=True)
    centred = source - average
    variance = jnp.mean(centred * centred, axis=-1, keepdims=True)
    return centred * lax.rsqrt(variance + eps_norm) * gain_vec + shift_vec


def gelu_tanh(values):
    return jax.nn.gelu(values, approximate=True)


def swap(values, axis, mask):
    count = lax.axis_size(axis)
    return lax.ppermute(values, axis, [(i, i ^ mask) for i in range(count)])


def spread_rows(shard):
    count = lax.axis_size("fsdp")
    spot = lax.axis_index("fsdp")
    rows, cols = shard.shape
    held = shard[None]
    mask = count // 2
    while mask:
        other = swap(held, "fsdp", mask)
        upper = (spot & mask) != 0
        held = jnp.where(upper, jnp.stack([other, held], 1), jnp.stack([held, other], 1))
        held = held.reshape(-1, rows, cols)
        mask //= 2
    return held.reshape(-1, cols)


def collect_rows(terms):
    count = lax.axis_size("fsdp")
    spot = lax.axis_index("fsdp")
    rows, cols = terms.shape
    held = terms
    mask = 1
    while mask < count:
        held = held.reshape(-1, 2, rows // count, cols)
        bit = jnp.where((spot & mask) != 0, 1, 0)
        kept = lax.dynamic_index_in_dim(held, bit, 1, keepdims=False)
        sent = lax.dynamic_index_in_dim(held, 1 - bit, 1, keepdims=False)
        held = kept + swap(sent.astype(LOW), "fsdp", mask).astype(F32)
        mask *= 2
    return held.reshape(-1, cols)


def total_over(values, axes):
    for axis in axes:
        mask = 1
        while mask < lax.axis_size(axis):
            values = values + swap(values, axis, mask)
            mask *= 2
    return values


def on_device(
    hidden_in,
    cotangent,
    norm1_gain,
    norm1_bias,
    w_query,
    w_key,
    w_value,
    w_out,
    norm2_gain,
    norm2_bias,
    w_fc1,
    bias_fc1,
    w_fc2,
    bias_fc2,
    segments,
    random_blocks,
):
    rows_dev, width_model = hidden_in.shape
    heads_wide = w_query.shape[1]
    rank = lax.axis_index("tp")
    seq_segs = segments[0]
    picks = random_blocks[0]
    heads_local = picks.shape[0]
    own_segs = lax.dynamic_slice_in_dim(seq_segs, rank * rows_dev, rows_dev)
    valid_rows = (own_segs != 0).astype(F32)[:, None]
    gain_first = norm1_gain.astype(F32)
    shift_first = norm1_bias.astype(F32)
    gain_second = norm2_gain.astype(F32)
    shift_second = norm2_bias.astype(F32)
    residual_in = hidden_in.astype(F32)
    scale_query = HEAD_DIM ** (-0.5)
    rank_word = rank.astype(jnp.int32).reshape(1)
    marks = token_marks(seq_segs, heads_local)

    w_qkv = spread_rows(jnp.concatenate([w_query * jnp.asarray(scale_query, LOW), w_key, w_value], 1))
    wo_own = spread_rows(w_out.T)
    wo_far = swap(wo_own, "tp", 2)
    wo_all = jnp.concatenate([wo_own, swap(wo_own, "tp", 1), wo_far, swap(wo_far, "tp", 1)], 1)
    w_up = [spread_rows(w_fc1), spread_rows(swap(w_fc1, "tp", 2))]
    w_down_local = w_fc2.T
    w_down = [spread_rows(w_down_local), spread_rows(swap(w_down_local, "tp", 2))]
    bias_up = [bias_fc1.astype(F32), swap(bias_fc1, "tp", 2).astype(F32)]

    normed_first, norm_first_back = jax.vjp(norm_rows, residual_in, gain_first, shift_first)
    first_own = normed_first.astype(LOW)
    first_far = swap(first_own, "tp", 2)
    first_all = jnp.concatenate(
        [first_own, swap(first_own, "tp", 1), first_far, swap(first_far, "tp", 1)], 0
    )
    qkv = dot_nn(first_all, w_qkv).astype(LOW)
    context = attend(rank_word, picks, qkv, marks)
    context_cat = jnp.concatenate(
        [context[:rows_dev]]
        + [swap(context[k * rows_dev : (k + 1) * rows_dev], "tp", k) for k in (1, 2, 3)],
        1,
    )
    attn_branch = dot_nt(context_cat, wo_all)
    middle = residual_in + attn_branch
    normed_second, norm_second_back = jax.vjp(norm_rows, middle, gain_second, shift_second)
    second_own = normed_second.astype(LOW)

    second_two = jnp.concatenate([second_own, swap(second_own, "tp", 1)], 0)
    grad_two = jnp.concatenate([cotangent, swap(cotangent, "tp", 1)], 0)
    hidden = []
    grad_pre = []
    for half in range(2):
        pre_act = dot_nn(second_two, w_up[half]) + bias_up[half]
        hidden_act, gelu_back = jax.vjp(gelu_tanh, pre_act)
        hidden.append(hidden_act.astype(LOW))
        grad_pre.append(gelu_back(dot_nn(grad_two, w_down[half]))[0].astype(LOW))
    second_terms = (dot_nt(grad_pre[0], w_up[0]) + dot_nt(grad_pre[1], w_up[1]))
    grad_normed_second = second_terms[:rows_dev] + swap(second_terms[rows_dev:].astype(LOW), "tp", 1).astype(F32)
    grad_branch = cotangent.astype(F32)
    grad_mid_norm, grad_gain_second, grad_shift_second = norm_second_back(grad_normed_second)
    grad_middle = grad_branch + grad_mid_norm

    grad_attn = grad_middle.astype(LOW)
    grad_context_cat = dot_nn(grad_attn, wo_all).astype(LOW)
    grad_context = jnp.concatenate(
        [grad_context_cat[:, :heads_wide]]
        + [swap(grad_context_cat[:, k * heads_wide : (k + 1) * heads_wide], "tp", k) for k in (1, 2, 3)],
        0,
    )

    down_terms = dot_nt(hidden[0], w_down[0]) + dot_nt(hidden[1], w_down[1])
    ffn_branch = (
        down_terms[:rows_dev]
        + swap(down_terms[rows_dev:].astype(LOW), "tp", 1).astype(F32)
        + bias_fc2.astype(F32)
    )
    output_rows = middle + ffn_branch
    up_terms = [collect_rows(dot_tn(second_two, grad_pre[half])) for half in range(2)]
    down_grads = [collect_rows(dot_tn(grad_two, hidden[half])) for half in range(2)]
    grad_w_up = up_terms[0] + swap(up_terms[1].astype(LOW), "tp", 2).astype(F32)
    grad_w_down = (down_grads[0] + swap(down_grads[1].astype(LOW), "tp", 2).astype(F32)).T
    bias_terms = [jnp.sum(grad_pre[half], axis=0, dtype=F32) for half in range(2)]
    grad_bias_up = bias_terms[0] + swap(bias_terms[1], "tp", 2)
    out_terms = dot_tn(grad_attn, context_cat)
    out_near = [out_terms[:, k * heads_wide : (k + 1) * heads_wide] for k in range(4)]
    out_chip = [
        out_near[k] + swap(out_near[k + 1].astype(LOW), "tp", 1).astype(F32) for k in (0, 2)
    ]
    out_sum = out_chip[0] + swap(out_chip[1].astype(LOW), "tp", 2).astype(F32)
    grad_w_o = collect_rows(out_sum).T

    grad_qkv = attend_back(rank_word, picks, qkv, grad_context, marks)
    far_terms = dot_nt(grad_qkv[2 * rows_dev :], w_qkv)
    near_terms = dot_nt(grad_qkv[: 2 * rows_dev], w_qkv)
    far_sum = far_terms[:rows_dev] + swap(far_terms[rows_dev:].astype(LOW), "tp", 1).astype(F32)
    grad_normed_first = (
        near_terms[:rows_dev]
        + swap(near_terms[rows_dev:].astype(LOW), "tp", 1).astype(F32)
        + swap(far_sum.astype(LOW), "tp", 2).astype(F32)
    )
    grad_w_qkv = collect_rows(dot_tn(first_all, grad_qkv))
    grad_w_q = grad_w_qkv[:, :heads_wide] * scale_query
    grad_w_k = grad_w_qkv[:, heads_wide : 2 * heads_wide]
    grad_w_v = grad_w_qkv[:, 2 * heads_wide :]
    grad_in_norm, grad_gain_first, grad_shift_first = norm_first_back(grad_normed_first)
    grad_input = grad_middle + grad_in_norm

    square_sums = jnp.stack(
        [
            jnp.sum(valid_rows * branch * branch)
            for branch in (residual_in, attn_branch, middle, ffn_branch)
        ]
        + [jnp.sum(valid_rows)]
    )
    early = jnp.concatenate(
        [grad_gain_second, grad_shift_second, jnp.sum(grad_branch, axis=0), square_sums]
    )
    early = total_over(early, ("tp",))
    early_size = early.shape[0]
    early = total_over(jnp.concatenate([early, grad_bias_up]), ("fsdp",))
    late = total_over(jnp.concatenate([grad_gain_first, grad_shift_first]), ("tp", "fsdp"))
    square_sums = early[3 * width_model : early_size]
    residual_rms = jnp.sqrt(square_sums[:4] / (square_sums[4] * width_model))
    return (
        output_rows.astype(LOW),
        grad_input,
        late[:width_model],
        late[width_model:],
        grad_w_q,
        grad_w_k,
        grad_w_v,
        grad_w_o,
        early[:width_model],
        early[width_model : 2 * width_model],
        grad_w_up,
        early[early_size:],
        grad_w_down,
        early[2 * width_model : 3 * width_model],
        residual_rms,
    )


def solution(mesh):
    in_specs = (
        P(("fsdp", "tp"), None),
        P(("fsdp", "tp"), None),
        P(),
        P(),
        P("fsdp", "tp"),
        P("fsdp", "tp"),
        P("fsdp", "tp"),
        P("tp", "fsdp"),
        P(),
        P(),
        P("fsdp", "tp"),
        P("tp"),
        P("tp", "fsdp"),
        P(),
        P("fsdp", None),
        P("fsdp", "tp", None, None),
    )
    out_specs = (
        P(("fsdp", "tp"), None),
        P(("fsdp", "tp"), None),
        P(),
        P(),
        P("fsdp", "tp"),
        P("fsdp", "tp"),
        P("fsdp", "tp"),
        P("tp", "fsdp"),
        P(),
        P(),
        P("fsdp", "tp"),
        P("tp"),
        P("tp", "fsdp"),
        P(),
        P(),
    )
    return jax.shard_map(
        on_device, mesh=mesh, in_specs=in_specs, out_specs=out_specs, check_vma=False
    )
```

```python
from functools import partial
import jax, jax.numpy as jnp
from jax import lax
from jax.experimental import pallas as pl
from jax.experimental.layout import Layout, with_layout_constraint
from jax.experimental.pallas import tpu as pltpu
from jax.sharding import PartitionSpec as P

HEAD_DIM = 64
BLOCK = 64
LANES = 128
F32 = jnp.float32
LOW = jnp.bfloat16
neg_large = -1e30


def dot_nn(a, b):
    return lax.dot_general(a, b, (((1,), (0,)), ((), ())), preferred_element_type=F32)


def dot_nt(a, b):
    return lax.dot_general(a, b, (((1,), (1,)), ((), ())), preferred_element_type=F32)


def dot_tn(a, b):
    return lax.dot_general(a, b, (((0,), (0,)), ((), ())), preferred_element_type=F32)


class Walk:
    def __init__(self, rank_ref, pick_ref, heads, seq, rand):
        self.rank = rank_ref[0]
        self.pick_ref = pick_ref
        self.heads = heads
        self.rand = rand
        self.nblocks = seq // BLOCK

    def place(self, blk):
        per = self.nblocks // 4
        chunk = lax.bitwise_xor(lax.div(blk, per), self.rank)
        return pl.multiple_of((chunk * per + lax.rem(blk, per)) * BLOCK, BLOCK)

    def span_of(self, near):
        upper = lax.div(self.rank, 2)
        half = upper if near else 1 - upper
        count = self.nblocks // 2 - 1
        return 1 + half * count, count, half * (self.nblocks - 1)

    def picked(self, blk, head, slot):
        return self.pick_ref[(head * (self.nblocks - 2) + blk - 1) * self.rand + slot]


def left_lanes(rows):
    return lax.broadcasted_iota(jnp.int32, (rows, LANES), 1) < HEAD_DIM


def spread_heads(rows, heads):
    tall = jnp.concatenate([rows.astype(F32)] * heads, axis=0)
    width = heads * HEAD_DIM
    row_head = lax.broadcasted_iota(jnp.int32, (heads * BLOCK, width), 0) // BLOCK
    col_head = lax.broadcasted_iota(jnp.int32, (heads * BLOCK, width), 1) // HEAD_DIM
    return jnp.where(row_head == col_head, tall, 0.0).astype(LOW)


def own_heads(full, heads):
    left = left_lanes(BLOCK)
    halves = []
    for pair in range(heads // 2):
        cols = slice(pair * LANES, (pair + 1) * LANES)
        first = full[2 * pair * BLOCK : (2 * pair + 1) * BLOCK, cols]
        second = full[(2 * pair + 1) * BLOCK : (2 * pair + 2) * BLOCK, cols]
        halves.append(jnp.where(left, first, second))
    return jnp.concatenate(halves, axis=1)


def gather_rows(ref, base, walk, blk):
    heads = walk.heads
    width = heads * HEAD_DIM
    left = left_lanes(BLOCK)
    parts = [
        ref[pl.ds(walk.place(at), BLOCK), base : base + width]
        for at in (blk - 1, blk, blk + 1, 0, walk.nblocks - 1)
    ]
    for slot in range(walk.rand):
        halves = []
        for pair in range(heads // 2):
            cols = slice(base + pair * LANES, base + (pair + 1) * LANES)
            first = ref[pl.ds(walk.place(walk.picked(blk, 2 * pair, slot)), BLOCK), cols]
            second = ref[pl.ds(walk.place(walk.picked(blk, 2 * pair + 1, slot)), BLOCK), cols]
            halves.append(jnp.where(left, first, second))
        parts.append(jnp.concatenate(halves, axis=1))
    return jnp.concatenate(parts, axis=0)


def key_marks(mark_ref, walk, blk):
    heads = walk.heads
    left = left_lanes(BLOCK)

    def rows_at(at):
        return mark_ref[pl.ds(pl.multiple_of(at * BLOCK, BLOCK), BLOCK), :]

    before = jnp.where(blk == 1, -1, rows_at(blk - 1))
    after = jnp.where(blk == walk.nblocks - 2, -1, rows_at(blk + 1))
    parts = [
        jnp.concatenate([rows] * (heads // 2), axis=1)
        for rows in (before, rows_at(blk), after, rows_at(0), rows_at(walk.nblocks - 1))
    ]
    for slot in range(walk.rand):
        halves = []
        for pair in range(heads // 2):
            first = rows_at(walk.picked(blk, 2 * pair, slot))
            second = rows_at(walk.picked(blk, 2 * pair + 1, slot))
            halves.append(jnp.where(left, first, second))
        parts.append(jnp.concatenate(halves, axis=1))
    return jnp.concatenate(parts, axis=0)


def chunk_marks(mark_ref, walk, at, size):
    per = walk.nblocks // 4 * BLOCK
    chunk = lax.bitwise_xor(lax.div(at, per), walk.rank)
    natural = pl.multiple_of(chunk * per + lax.rem(at, per), BLOCK)
    rows = mark_ref[pl.ds(natural, size), :]
    return jnp.concatenate([rows] * (walk.heads // 2), axis=1)


def forward_kernel(rank_ref, pick_ref, qkv_ref, mark_ref, qmark_ref, out_ref, score_ref, *, heads, rand, span, near):
    seq = qkv_ref.shape[0]
    width = heads * HEAD_DIM
    walk = Walk(rank_ref, pick_ref, heads, seq, rand)
    first, count, dense = walk.span_of(near)
    base = 0 if near else seq // 2

    def middle(blk):
        place = walk.place(blk)
        query = spread_heads(qkv_ref[pl.ds(place, BLOCK), 0:width], heads)
        keys = gather_rows(qkv_ref, width, walk, blk)
        score = dot_nt(keys, query)
        ok = key_marks(mark_ref, walk, blk) == qmark_ref[pl.ds(blk, 1), :]
        score = jnp.where(ok, score, neg_large)
        expo = jnp.exp(score - jnp.max(score, axis=0, keepdims=True))
        probs = (expo * (1.0 / jnp.sum(expo, axis=0, keepdims=True))).astype(LOW)
        values = gather_rows(qkv_ref, 2 * width, walk, blk)
        out_ref[pl.ds(pl.multiple_of(place - base, BLOCK), BLOCK), :] = own_heads(dot_tn(probs, values), heads).astype(LOW)

    def pair(step, carry):
        middle(first + 2 * step)
        middle(first + 2 * step + 1)
        return carry

    lax.fori_loop(0, count // 2, pair, 0)
    for extra in range(count - count % 2, count):
        middle(first + extra)

    place = walk.place(dense)
    query = spread_heads(qkv_ref[pl.ds(place, BLOCK), 0:width], heads)
    qmark = qmark_ref[pl.ds(dense, 1), :]

    def scores_at(step, top):
        at = pl.multiple_of(step * span, span)
        score = dot_nt(qkv_ref[pl.ds(at, span), width : 2 * width], query)
        score = jnp.where(chunk_marks(mark_ref, walk, at, span) == qmark, score, neg_large)
        score_ref[pl.ds(at, span), :] = score
        return jnp.maximum(top, jnp.max(score, axis=0, keepdims=True))

    def expo_at(step, total, top):
        at = pl.multiple_of(step * span, span)
        expo = jnp.exp(score_ref[pl.ds(at, span), :] - top)
        score_ref[pl.ds(at, span), :] = expo
        return total + jnp.sum(expo, axis=0, keepdims=True)

    def value_at(step, total, scale):
        at = pl.multiple_of(step * span, span)
        probs = (score_ref[pl.ds(at, span), :] * scale).astype(LOW)
        return total + dot_tn(probs, qkv_ref[pl.ds(at, span), 2 * width : 3 * width])

    top = jnp.full((1, heads * BLOCK), neg_large, F32)
    top = lax.fori_loop(0, seq // span, scores_at, top)
    total = lax.fori_loop(0, seq // span, partial(expo_at, top=top), jnp.zeros_like(top))
    full = lax.fori_loop(0, seq // span, partial(value_at, scale=1.0 / total), jnp.zeros((heads * BLOCK, width), F32))
    out_ref[pl.ds(pl.multiple_of(place - base, BLOCK), BLOCK), :] = own_heads(full, heads).astype(LOW)


def backward_body(rank_ref, pick_ref, qkv_ref, grad_ref, mark_ref, qmark_ref, query_ref, key_acc, value_acc, score_ref, dprob_ref, heads, rand, span, near):
    seq = qkv_ref.shape[0]
    width = heads * HEAD_DIM
    walk = Walk(rank_ref, pick_ref, heads, seq, rand)
    left = left_lanes(BLOCK)

    first, count, dense = walk.span_of(near)
    base = 0 if near else seq // 2

    def add_rows(acc, rows, blk):
        for index, at in enumerate((blk - 1, blk, blk + 1, 0, walk.nblocks - 1)):
            acc[pl.ds(walk.place(at), BLOCK), :] += rows[index * BLOCK : (index + 1) * BLOCK, :]
        for slot in range(rand):
            row = (5 + slot) * BLOCK
            for pair in range(heads // 2):
                cols = slice(pair * LANES, (pair + 1) * LANES)
                piece = rows[row : row + BLOCK, cols]
                acc[pl.ds(walk.place(walk.picked(blk, 2 * pair, slot)), BLOCK), cols] += jnp.where(left, piece, 0.0)
                acc[pl.ds(walk.place(walk.picked(blk, 2 * pair + 1, slot)), BLOCK), cols] += jnp.where(left, 0.0, piece)

    def middle(blk):
        place = walk.place(blk)
        query = spread_heads(qkv_ref[pl.ds(place, BLOCK), 0:width], heads)
        half_row = pl.multiple_of(place - base, BLOCK)
        grad = spread_heads(grad_ref[pl.ds(half_row, BLOCK), :], heads)
        keys = gather_rows(qkv_ref, width, walk, blk)
        values = gather_rows(qkv_ref, 2 * width, walk, blk)
        score = dot_nt(keys, query)
        ok = key_marks(mark_ref, walk, blk) == qmark_ref[pl.ds(blk, 1), :]
        score = jnp.where(ok, score, neg_large)
        expo = jnp.exp(score - jnp.max(score, axis=0, keepdims=True))
        probs = expo * (1.0 / jnp.sum(expo, axis=0, keepdims=True))
        dprob = dot_nt(values, grad)
        delta = jnp.sum(probs * dprob, axis=0, keepdims=True)
        dscore = (probs * (dprob - delta)).astype(LOW)
        dvalue = dot_nn(probs.astype(LOW), grad)
        dkey = dot_nn(dscore, query)
        dquery = own_heads(dot_tn(dscore, keys), heads)
        query_ref[pl.ds(half_row if near else place, BLOCK), 0:width] = dquery.astype(LOW)
        return dkey, dvalue

    def pair(step, carry):
        blk = first + 2 * step
        dkey_a, dvalue_a = middle(blk)
        dkey_b, dvalue_b = middle(blk + 1)
        add_rows(key_acc, dkey_a, blk)
        add_rows(value_acc, dvalue_a, blk)
        add_rows(key_acc, dkey_b, blk + 1)
        add_rows(value_acc, dvalue_b, blk + 1)
        return carry

    lax.fori_loop(0, count // 2, pair, 0)
    for extra in range(count - count % 2, count):
        dkey, dvalue = middle(first + extra)
        add_rows(key_acc, dkey, first + extra)
        add_rows(value_acc, dvalue, first + extra)

    place = walk.place(dense)
    half_row = pl.multiple_of(place - base, BLOCK)
    query = spread_heads(qkv_ref[pl.ds(place, BLOCK), 0:width], heads)
    grad = spread_heads(grad_ref[pl.ds(half_row, BLOCK), :], heads)
    qmark = qmark_ref[pl.ds(dense, 1), :]

    def scores_at(step, top):
        at = pl.multiple_of(step * span, span)
        score = dot_nt(qkv_ref[pl.ds(at, span), width : 2 * width], query)
        score = jnp.where(chunk_marks(mark_ref, walk, at, span) == qmark, score, neg_large)
        score_ref[pl.ds(at, span), :] = score
        dprob_ref[pl.ds(at, span), :] = dot_nt(qkv_ref[pl.ds(at, span), 2 * width : 3 * width], grad)
        return jnp.maximum(top, jnp.max(score, axis=0, keepdims=True))

    def expo_at(step, carry, top):
        total, weighted = carry
        at = pl.multiple_of(step * span, span)
        expo = jnp.exp(score_ref[pl.ds(at, span), :] - top)
        score_ref[pl.ds(at, span), :] = expo
        return (
            total + jnp.sum(expo, axis=0, keepdims=True),
            weighted + jnp.sum(expo * dprob_ref[pl.ds(at, span), :], axis=0, keepdims=True),
        )

    def grads_at(step, dquery, scale, delta):
        at = pl.multiple_of(step * span, span)
        probs = score_ref[pl.ds(at, span), :] * scale
        dscore = (probs * (dprob_ref[pl.ds(at, span), :] - delta)).astype(LOW)
        value_acc[pl.ds(at, span), :] += dot_nn(probs.astype(LOW), grad)
        key_acc[pl.ds(at, span), :] += dot_nn(dscore, query)
        return dquery + dot_tn(dscore, qkv_ref[pl.ds(at, span), width : 2 * width])

    top = jnp.full((1, heads * BLOCK), neg_large, F32)
    top = lax.fori_loop(0, seq // span, scores_at, top)
    total, weighted = lax.fori_loop(0, seq // span, partial(expo_at, top=top), (jnp.zeros_like(top), jnp.zeros_like(top)))
    scale = 1.0 / total
    full = lax.fori_loop(0, seq // span, partial(grads_at, scale=scale, delta=weighted * scale), jnp.zeros((heads * BLOCK, width), F32))
    query_ref[pl.ds(half_row if near else place, BLOCK), 0:width] = own_heads(full, heads).astype(LOW)


def backward_near(rank_ref, pick_ref, qkv_ref, grad_ref, mark_ref, qmark_ref, query_ref, key_acc, value_acc, score_ref, dprob_ref, *, heads, rand, span):
    seq = qkv_ref.shape[0]
    width = heads * HEAD_DIM

    def clear(step, carry):
        at = pl.multiple_of(step * span, span)
        key_acc[pl.ds(at, span), :] = jnp.zeros((span, width), F32)
        value_acc[pl.ds(at, span), :] = jnp.zeros((span, width), F32)
        return carry

    lax.fori_loop(0, seq // span, clear, 0)
    backward_body(rank_ref, pick_ref, qkv_ref, grad_ref, mark_ref, qmark_ref, query_ref, key_acc, value_acc, score_ref, dprob_ref, heads, rand, span, True)


def backward_far(rank_ref, pick_ref, qkv_ref, grad_ref, mark_ref, qmark_ref, near_ref, key_in, value_in, out_ref, key_acc, value_acc, score_ref, dprob_ref, *, heads, rand, span):
    seq = qkv_ref.shape[0]
    width = heads * HEAD_DIM

    def begin(step, carry):
        at = pl.multiple_of(step * span, span)
        key_acc[pl.ds(at, span), :] = key_in[pl.ds(at, span), :]
        value_acc[pl.ds(at, span), :] = value_in[pl.ds(at, span), :]
        return carry

    lax.fori_loop(0, seq // span, begin, 0)
    out_ref[0 : seq // 2, 0:width] = near_ref[...]
    backward_body(rank_ref, pick_ref, qkv_ref, grad_ref, mark_ref, qmark_ref, out_ref, key_acc, value_acc, score_ref, dprob_ref, heads, rand, span, False)

    def finish(step, carry):
        at = pl.multiple_of(step * span, span)
        out_ref[pl.ds(at, span), width : 2 * width] = key_acc[pl.ds(at, span), :].astype(LOW)
        out_ref[pl.ds(at, span), 2 * width : 3 * width] = value_acc[pl.ds(at, span), :].astype(LOW)
        return carry

    lax.fori_loop(0, seq // span, finish, 0)


def token_marks(seq_segs, heads):
    seq = seq_segs.shape[0]
    marks = jnp.where(seq_segs != 0, seq_segs, 1000 + jnp.arange(seq, dtype=jnp.int32))
    by_row = jnp.broadcast_to(marks[:, None], (seq, LANES))
    by_block = jnp.tile(marks.reshape(seq // BLOCK, BLOCK), (1, heads))
    return by_row, by_block


def spent(micros):
    return pl.CostEstimate(flops=micros * 10**9, bytes_accessed=micros * 10**6, transcendentals=0)


SMEM_SPEC = pl.BlockSpec(memory_space=pltpu.SMEM)
VMEM_SPEC = pl.BlockSpec(memory_space=pltpu.VMEM)


def attend(rank, picks, qkv, marks, near):
    heads, _, rand = picks.shape
    seq = qkv.shape[0]
    width = heads * HEAD_DIM
    span = min(512, seq // 4)
    return pl.pallas_call(
        partial(forward_kernel, heads=heads, rand=rand, span=span, near=near),
        out_shape=jax.ShapeDtypeStruct((seq // 2, width), LOW),
        in_specs=[SMEM_SPEC, SMEM_SPEC, VMEM_SPEC, VMEM_SPEC, VMEM_SPEC],
        out_specs=VMEM_SPEC,
        scratch_shapes=[pltpu.VMEM((seq, heads * BLOCK), F32)],
        name="attend_near" if near else "attend_far",
        cost_estimate=spent(29),
    )(rank, picks.reshape(-1), qkv, *marks)


def attend_back_near(rank, picks, qkv, grad_context, marks):
    heads, _, rand = picks.shape
    seq = qkv.shape[0]
    width = heads * HEAD_DIM
    span = min(512, seq // 4)
    total = jax.ShapeDtypeStruct((seq, width), F32)
    return pl.pallas_call(
        partial(backward_near, heads=heads, rand=rand, span=span),
        out_shape=[jax.ShapeDtypeStruct((seq // 2, width), LOW), total, total],
        in_specs=[SMEM_SPEC, SMEM_SPEC, VMEM_SPEC, VMEM_SPEC, VMEM_SPEC, VMEM_SPEC],
        out_specs=[VMEM_SPEC] * 3,
        scratch_shapes=[pltpu.VMEM((seq, heads * BLOCK), F32)] * 2,
        name="attend_back_near",
        cost_estimate=spent(40),
    )(rank, picks.reshape(-1), qkv, grad_context, *marks)


def attend_back_far(rank, picks, qkv, grad_context, marks, near_parts):
    heads, _, rand = picks.shape
    seq = qkv.shape[0]
    width = heads * HEAD_DIM
    span = min(512, seq // 4)
    return pl.pallas_call(
        partial(backward_far, heads=heads, rand=rand, span=span),
        out_shape=jax.ShapeDtypeStruct((seq, 3 * width), LOW),
        in_specs=[SMEM_SPEC, SMEM_SPEC] + [VMEM_SPEC] * 7,
        out_specs=VMEM_SPEC,
        scratch_shapes=[pltpu.VMEM((seq, width), F32)] * 2 + [pltpu.VMEM((seq, heads * BLOCK), F32)] * 2,
        name="attend_back_far",
        cost_estimate=spent(43),
    )(rank, picks.reshape(-1), qkv, grad_context, *marks, *near_parts)


eps_norm = 1e-05


def by_rows(values):
    return with_layout_constraint(values, Layout(major_to_minor=(0, 1)))


def tie(values, *others):
    return lax.optimization_barrier((values, others))[0]


def norm_rows(source, gain_vec, shift_vec):
    average = jnp.mean(source, axis=-1, keepdims=True)
    centred = source - average
    variance = jnp.mean(centred * centred, axis=-1, keepdims=True)
    return centred * lax.rsqrt(variance + eps_norm) * gain_vec + shift_vec


def norm_kernel(source_ref, gain_ref, shift_ref, out_ref):
    source = source_ref[...].astype(F32)
    out_ref[...] = norm_rows(source, gain_ref[...], shift_ref[...]).astype(LOW)


def norm_call(source, gain, shift):
    rows, model = source.shape
    tile = min(256, rows)
    vector = pl.BlockSpec((1, model), lambda i: (0, 0))
    block = pl.BlockSpec((tile, model), lambda i: (i, 0))
    return pl.pallas_call(
        norm_kernel,
        grid=(rows // tile,),
        in_specs=[block, vector, vector],
        out_specs=block,
        out_shape=jax.ShapeDtypeStruct((rows, model), LOW),
        name="norm",
        cost_estimate=spent(3),
    )(source, gain, shift)


def norm_back_kernel(source_ref, gain_ref, residual_ref, *rest, terms, narrow):
    term_refs = rest[:terms]
    out_ref = rest[terms]
    low_ref = rest[terms + 1] if narrow else None
    sum_ref = rest[-1]
    source = source_ref[...].astype(F32)
    grad = term_refs[0][...].astype(F32)
    for ref in term_refs[1:]:
        grad = grad + ref[...].astype(F32)
    average = jnp.mean(source, axis=-1, keepdims=True)
    centred = source - average
    variance = jnp.mean(centred * centred, axis=-1, keepdims=True)
    scale = lax.rsqrt(variance + eps_norm)
    normal = centred * scale
    scaled = grad * gain_ref[...]
    first = jnp.mean(scaled, axis=-1, keepdims=True)
    second = jnp.mean(scaled * normal, axis=-1, keepdims=True)
    residual = residual_ref[...].astype(F32)
    full = residual + scale * (scaled - first - normal * second)
    out_ref[...] = full
    if narrow:
        low_ref[...] = full.astype(LOW)
    model = source.shape[1]
    parts = [jnp.sum(grad * normal, axis=0, keepdims=True), jnp.sum(grad, axis=0, keepdims=True)]
    if narrow:
        parts.append(jnp.sum(residual, axis=0, keepdims=True))
    parts.append(jnp.zeros((8 - len(parts), model), F32))
    parts = jnp.concatenate(parts, axis=0)

    @pl.when(pl.program_id(0) == 0)
    def _():
        sum_ref[...] = parts

    @pl.when(pl.program_id(0) != 0)
    def _():
        sum_ref[...] += parts


def norm_back(source, gain, residual, terms, narrow):
    rows, model = source.shape
    tile = min(256, rows)
    vector = pl.BlockSpec((1, model), lambda i: (0, 0))
    block = pl.BlockSpec((tile, model), lambda i: (i, 0))
    shapes = [jax.ShapeDtypeStruct((rows, model), F32)]
    if narrow:
        shapes.append(jax.ShapeDtypeStruct((rows, model), LOW))
    return pl.pallas_call(
        partial(norm_back_kernel, terms=len(terms), narrow=narrow),
        grid=(rows // tile,),
        in_specs=[block, vector] + [block] * (1 + len(terms)),
        out_specs=[block] * len(shapes) + [pl.BlockSpec((8, model), lambda i: (0, 0))],
        out_shape=shapes + [jax.ShapeDtypeStruct((8, model), F32)],
        name="norm_back",
        cost_estimate=spent(7),
    )(source, gain, residual, *terms)


def feed_kernel(second_own, second_side, grad_own, grad_side, up_ref, down_ref, bias_ref, hidden_ref, pre_ref, sum_ref, *, step):
    slope = (2.0 / jnp.pi) ** 0.5

    def run(second_ref, grad_ref):
        total = jnp.zeros(sum_ref.shape[1:], F32)
        for at in range(0, second_ref.shape[0], step):
            rows = slice(at, at + step)
            unit = dot_nn(second_ref[rows, :], up_ref[...]) + bias_ref[...]
            grad = dot_nn(grad_ref[rows, :], down_ref[...])
            square = unit * unit
            bent = jnp.tanh(unit * (slope + (slope * 0.044715) * square))
            half = 0.5 + 0.5 * bent
            hidden_ref[rows, :] = (unit * half).astype(LOW)
            rise = half + (0.5 * unit) * (1.0 - bent * bent) * (slope + (slope * 0.134145) * square)
            low = (grad * rise).astype(LOW)
            pre_ref[rows, :] = low
            total = total + jnp.sum(low.astype(F32), axis=0, keepdims=True)
        sum_ref[0] = total

    @pl.when(pl.program_id(0) == 0)
    def _():
        run(second_own, grad_own)

    @pl.when(pl.program_id(0) == 1)
    def _():
        run(second_side, grad_side)


def feed(seconds, grads, weights, first_up, first_down, bias):
    rows, model = seconds[0].shape
    units = bias.shape[0]
    tile = min(256, units)
    whole = pl.BlockSpec((rows, model), lambda t, u: (0, 0))
    out = pl.BlockSpec((rows, tile), lambda t, u: (t, u))
    return pl.pallas_call(
        partial(feed_kernel, step=min(256, rows)),
        grid=(2, units // tile),
        in_specs=[whole] * 4
        + [
            pl.BlockSpec((model, tile), lambda t, u: (0, first_up // tile + u)),
            pl.BlockSpec((model, tile), lambda t, u: (0, first_down // tile + u)),
            pl.BlockSpec((1, tile), lambda t, u: (0, u)),
        ],
        out_specs=[out, out, pl.BlockSpec((1, 1, tile), lambda t, u: (t, 0, u))],
        out_shape=[
            jax.ShapeDtypeStruct((2 * rows, units), LOW),
            jax.ShapeDtypeStruct((2 * rows, units), LOW),
            jax.ShapeDtypeStruct((2, 1, units), F32),
        ],
        name="feed",
        cost_estimate=spent(14),
    )(*seconds, *grads, weights, weights, bias[None])


def swap(values, axis, mask):
    count = lax.axis_size(axis)
    return lax.ppermute(values, axis, [(i, i ^ mask) for i in range(count)])


def collect_rows(parts, gate):
    count = lax.axis_size("fsdp")
    spot = lax.axis_index("fsdp")
    rows = parts[0].shape[0] // count
    mask = 1
    while mask < count:
        upper = (spot & mask) != 0
        parts = [part.reshape(-1, 2, rows, part.shape[-1]) for part in parts]
        sent = [jnp.where(upper, part[:, 0], part[:, 1]).astype(LOW) for part in parts]
        got = swap(jnp.concatenate(sent, -1), "fsdp", mask)
        first = 0
        held = []
        for part in parts:
            last = first + part.shape[-1]
            held.append(jnp.where(upper, part[:, 1], part[:, 0]) + got[..., first:last].astype(F32))
            first = last
        parts = held
        if mask == 1:
            parts, gate = lax.optimization_barrier((parts, gate))
        mask *= 2
    return [part.reshape(rows, part.shape[-1]) for part in parts], gate


def total_over(values, axis):
    bits = [1 << k for k in range(lax.axis_size(axis).bit_length() - 1)]
    while bits:
        if len(bits) % 2:
            values = values + swap(values, axis, bits.pop(0))
        else:
            low, high = bits.pop(0), bits.pop(0)
            values = (values + swap(values, axis, low)) + (swap(values, axis, high) + swap(values, axis, low | high))
    return values


def on_device(
    hidden_in,
    cotangent,
    norm1_gain,
    norm1_bias,
    w_query,
    w_key,
    w_value,
    w_out,
    norm2_gain,
    norm2_bias,
    w_fc1,
    bias_fc1,
    w_fc2,
    bias_fc2,
    segments,
    random_blocks,
):
    rows_dev, width_model = hidden_in.shape
    heads_wide = w_query.shape[1]
    rank = lax.axis_index("tp")
    seq_segs = segments[0]
    picks = random_blocks[0]
    heads_local = picks.shape[0]
    own_segs = lax.dynamic_slice_in_dim(seq_segs, rank * rows_dev, rows_dev)
    valid_rows = (own_segs != 0).astype(F32)[:, None]
    gain_first = norm1_gain.astype(F32)[None]
    shift_first = norm1_bias.astype(F32)[None]
    gain_second = norm2_gain.astype(F32)[None]
    shift_second = norm2_bias.astype(F32)[None]
    residual_in = hidden_in.astype(F32)
    scale_query = HEAD_DIM ** (-0.5)
    rank_word = rank.astype(jnp.int32).reshape(1)
    marks = token_marks(seq_segs, heads_local)

    heads_local_w = by_rows(jnp.concatenate([w_query * jnp.asarray(scale_query, LOW), w_key, w_value, w_out.T], 1))
    w_heads = lax.all_gather(heads_local_w, "fsdp", axis=0, tiled=True)
    pair_local = by_rows(jnp.concatenate([w_fc1, w_fc2.T], 1))
    units = w_fc1.shape[1]
    own_all = lax.all_gather(pair_local, "fsdp", axis=0, tiled=True)
    far_hidden = swap(hidden_in, "tp", 2)
    far_local = swap(tie(pair_local, far_hidden), "tp", 2)
    bias_up = [bias_fc1.astype(F32), swap(bias_fc1, "tp", 2).astype(F32)]

    first_own = norm_call(tie(hidden_in, marks, picks), gain_first, shift_first)
    first_side = swap(first_own, "tp", 1)
    far_hidden, w_heads = lax.optimization_barrier((far_hidden, w_heads))
    w_qkv = w_heads[:, : 3 * heads_wide]
    first_far = norm_call(far_hidden, gain_first, shift_first)
    first_cross = swap(first_far, "tp", 1)
    chunks = (first_own, first_side, first_far, first_cross)
    qkv = jnp.concatenate([dot_nn(chunk, w_qkv).astype(LOW) for chunk in chunks], 0)
    qkv, far_local = lax.optimization_barrier((qkv, far_local))
    far_all = lax.all_gather(far_local, "fsdp", axis=0, tiled=True)
    context_far = attend(rank_word, picks, qkv, marks, False)
    context_cross = [swap(context_far[k * rows_dev : (k + 1) * rows_dev], "tp", 2 + k) for k in (0, 1)]
    wo_own = tie(w_heads, qkv)[:, 3 * heads_wide :]
    wo_pair = jnp.concatenate([wo_own, swap(wo_own, "tp", 2)], 1)
    wo_side = swap(wo_pair, "tp", 1)
    wo_all = by_rows(jnp.concatenate(
        [wo_pair[:, :heads_wide], wo_side[:, :heads_wide], wo_pair[:, heads_wide:], wo_side[:, heads_wide:]], 1
    ))
    context_near = attend(rank_word, picks, tie(qkv, context_far), marks, True)
    side_context, context_cross = lax.optimization_barrier((context_near[rows_dev:], context_cross))
    context_cat = by_rows(jnp.concatenate(
        [context_near[:rows_dev], swap(side_context, "tp", 1)] + context_cross, 1
    ))
    attn_branch = by_rows(dot_nt(context_cat, wo_all))
    middle = residual_in + attn_branch
    second_own = by_rows(norm_rows(middle, gain_second, shift_second).astype(LOW))
    w_up = [own_all[:, :units], far_all[:, :units]]
    w_down = [own_all[:, units:], far_all[:, units:]]

    second_side = swap(second_own, "tp", 1)
    grad_side = swap(cotangent, "tp", 1)
    hidden, grad_pre, bias_parts = zip(
        feed((second_own, second_side), (cotangent, grad_side), own_all, 0, units, bias_up[0]),
        feed((second_own, second_side), (cotangent, grad_side), far_all, 0, units, bias_up[1]),
    )
    side_terms = dot_nt(grad_pre[0][rows_dev:], w_up[0]) + dot_nt(grad_pre[1][rows_dev:], w_up[1])
    side_back = swap(by_rows(side_terms.astype(LOW)), "tp", 1)
    own_terms = dot_nt(grad_pre[0][:rows_dev], w_up[0]) + dot_nt(grad_pre[1][:rows_dev], w_up[1])
    second_two = jnp.concatenate([second_own, second_side], 0)
    grad_two = jnp.concatenate([cotangent, grad_side], 0)
    share = by_rows(jnp.concatenate(
        [dot_tn(second_two, grad_pre[half]).astype(LOW) for half in range(2)]
        + [dot_tn(grad_two, hidden[half]).astype(LOW) for half in range(2)],
        1,
    ))
    grad_middle, grad_attn, second_sums = norm_back(middle, gain_second, cotangent, (by_rows(own_terms), side_back), True)

    grad_context_cat = dot_nn(grad_attn, wo_all).astype(LOW)
    grad_parts = [grad_context_cat[:, k * heads_wide : (k + 1) * heads_wide] for k in range(4)]
    grad_far = jnp.concatenate([swap(grad_parts[2], "tp", 2), swap(grad_parts[3], "tp", 3)], 0)
    grad_near = jnp.concatenate([grad_parts[0], swap(grad_parts[1], "tp", 1)], 0)
    out_terms = by_rows(dot_tn(grad_attn, context_cat))
    out_near = [out_terms[:, k * heads_wide : (k + 1) * heads_wide] for k in range(4)]
    out_chip = [
        out_near[k] + swap(out_near[k + 1].astype(LOW), "tp", 1).astype(F32) for k in (0, 2)
    ]
    out_sum = out_chip[0] + swap(out_chip[1].astype(LOW), "tp", 2).astype(F32)
    grad_near, share, out_terms = lax.optimization_barrier((grad_near, share, out_terms))
    share = lax.psum_scatter(share, "fsdp", scatter_dimension=0, tiled=True)
    near_parts = attend_back_near(rank_word, picks, qkv, grad_near, marks)
    out_sum, grad_far, near_parts = lax.optimization_barrier((out_sum, grad_far, near_parts))
    grad_qkv = attend_back_far(rank_word, picks, qkv, grad_far, marks, near_parts)
    far_side = by_rows(dot_nt(grad_qkv[3 * rows_dev :], w_qkv).astype(LOW))
    far_own = by_rows(dot_nt(grad_qkv[2 * rows_dev : 3 * rows_dev], w_qkv))
    far_side, far_own = lax.optimization_barrier((swap(far_side, "tp", 1), far_own))
    far_low = (far_own + far_side.astype(F32)).astype(LOW)
    far_back = swap(far_low, "tp", 2)

    hidden = tie(hidden, far_low)
    grad_qkv_late = tie(grad_qkv, far_low)
    qkv_terms = by_rows(dot_tn(jnp.concatenate(chunks, 0), grad_qkv_late))
    near_side = by_rows(dot_nt(grad_qkv_late[rows_dev : 2 * rows_dev], w_qkv).astype(LOW))
    near_own = by_rows(dot_nt(grad_qkv_late[:rows_dev], w_qkv))
    near_back = swap(near_side, "tp", 1)
    down_side = dot_nt(hidden[0][rows_dev:], w_down[0]) + dot_nt(hidden[1][rows_dev:], w_down[1])
    down_own = dot_nt(hidden[0][:rows_dev], w_down[0]) + dot_nt(hidden[1][:rows_dev], w_down[1])
    down_back = swap(by_rows(down_side.astype(LOW)), "tp", 1)
    ffn_branch = by_rows(down_own) + down_back.astype(F32) + bias_fc2.astype(F32)
    output_rows = by_rows((middle + ffn_branch).astype(LOW))
    bias_terms = [jnp.sum(parts, axis=0) for parts in bias_parts]
    grad_bias_up = bias_terms[0] + swap(bias_terms[1], "tp", 2)
    square_rows = jnp.stack(
        [
            jnp.sum(valid_rows * branch * branch)
            for branch in (residual_in, attn_branch, middle, ffn_branch)
        ]
        + [jnp.sum(valid_rows)]
    )
    square_rows = jnp.pad(square_rows[None], ((0, 0), (0, width_model - 5)))

    (collected, grad_w_o), (far_back, output_rows, square_rows, share, near_back) = collect_rows(
        [qkv_terms, out_sum], (far_back, output_rows, square_rows, share, near_back)
    )
    share = share.astype(F32)
    across = jnp.concatenate([share[:, units : 2 * units], share[:, 3 * units :]], 1)
    across = swap(across.astype(LOW), "tp", 2).astype(F32)
    grad_w_up = share[:, :units] + across[:, :units]
    grad_w_down = (share[:, 2 * units : 3 * units] + across[:, units:]).T
    grad_w_q = collected[:, :heads_wide] * scale_query
    grad_w_k = collected[:, heads_wide : 2 * heads_wide]
    grad_w_v = collected[:, 2 * heads_wide :]
    grad_w_o = grad_w_o.T
    grad_input, first_sums = norm_back(hidden_in, gain_first, grad_middle, (near_own, near_back, far_back), False)

    sums = jnp.concatenate([second_sums[:3], square_rows, first_sums[:2]])
    sums = total_over(sums, "tp")
    bias_rows = grad_bias_up.reshape(-1, width_model)
    sums = total_over(jnp.concatenate([sums, bias_rows]), "fsdp")
    residual_rms = jnp.sqrt(sums[3, :4] / (sums[3, 4] * width_model))
    return (
        output_rows,
        grad_input,
        sums[4],
        sums[5],
        grad_w_q,
        grad_w_k,
        grad_w_v,
        grad_w_o,
        sums[0],
        sums[1],
        grad_w_up,
        sums[6:].reshape(-1),
        grad_w_down,
        sums[2],
        residual_rms,
    )


def solution(mesh):
    in_specs = (
        P(("fsdp", "tp"), None),
        P(("fsdp", "tp"), None),
        P(),
        P(),
        P("fsdp", "tp"),
        P("fsdp", "tp"),
        P("fsdp", "tp"),
        P("tp", "fsdp"),
        P(),
        P(),
        P("fsdp", "tp"),
        P("tp"),
        P("tp", "fsdp"),
        P(),
        P("fsdp", None),
        P("fsdp", "tp", None, None),
    )
    out_specs = (
        P(("fsdp", "tp"), None),
        P(("fsdp", "tp"), None),
        P(),
        P(),
        P("fsdp", "tp"),
        P("fsdp", "tp"),
        P("fsdp", "tp"),
        P("tp", "fsdp"),
        P(),
        P(),
        P("fsdp", "tp"),
        P("tp"),
        P("tp", "fsdp"),
        P(),
        P(),
    )
    return jax.shard_map(
        on_device, mesh=mesh, in_specs=in_specs, out_specs=out_specs, check_vma=False
    )
```

```python
from functools import partial
import jax, jax.numpy as jnp
from jax import lax
from jax.experimental import pallas as pl
from jax.experimental.layout import Layout, with_layout_constraint
from jax.experimental.pallas import tpu as pltpu
from jax.sharding import PartitionSpec as P

HEAD_DIM = 64
BLOCK = 64
LANES = 128
F32 = jnp.float32
LOW = jnp.bfloat16
neg_large = -1e30
UNROLL = 5
UNROLL_FORWARD = 10


def dot_nn(a, b):
    return lax.dot_general(a, b, (((1,), (0,)), ((), ())), preferred_element_type=F32)


def dot_nt(a, b):
    return lax.dot_general(a, b, (((1,), (1,)), ((), ())), preferred_element_type=F32)


def dot_tn(a, b):
    return lax.dot_general(a, b, (((0,), (0,)), ((), ())), preferred_element_type=F32)


class Walk:
    def __init__(self, rank_ref, pick_ref, heads, seq, rand):
        self.rank = rank_ref[0]
        self.pick_ref = pick_ref
        self.heads = heads
        self.rand = rand
        self.nblocks = seq // BLOCK

    def place(self, blk):
        per = self.nblocks // 4
        chunk = lax.bitwise_xor(lax.div(blk, per), self.rank)
        return pl.multiple_of((chunk * per + lax.rem(blk, per)) * BLOCK, BLOCK)

    def span_of(self, near):
        upper = lax.div(self.rank, 2)
        half = upper if near else 1 - upper
        count = self.nblocks // 2 - 1
        return 1 + half * count, count, half * (self.nblocks - 1)

    def picked(self, blk, head, slot):
        return self.pick_ref[(head * (self.nblocks - 2) + blk - 1) * self.rand + slot]


def left_lanes(rows):
    return lax.broadcasted_iota(jnp.int32, (rows, LANES), 1) < HEAD_DIM


def spread_heads(rows, heads):
    tall = jnp.concatenate([rows.astype(F32)] * heads, axis=0)
    width = heads * HEAD_DIM
    row_head = lax.broadcasted_iota(jnp.int32, (heads * BLOCK, width), 0) // BLOCK
    col_head = lax.broadcasted_iota(jnp.int32, (heads * BLOCK, width), 1) // HEAD_DIM
    return jnp.where(row_head == col_head, tall, 0.0).astype(LOW)


def own_heads(full, heads):
    left = left_lanes(BLOCK)
    halves = []
    for pair in range(heads // 2):
        cols = slice(pair * LANES, (pair + 1) * LANES)
        first = full[2 * pair * BLOCK : (2 * pair + 1) * BLOCK, cols]
        second = full[(2 * pair + 1) * BLOCK : (2 * pair + 2) * BLOCK, cols]
        halves.append(jnp.where(left, first, second))
    return jnp.concatenate(halves, axis=1)


def gather_rows(ref, base, walk, blk):
    heads = walk.heads
    width = heads * HEAD_DIM
    left = left_lanes(BLOCK)
    parts = [
        ref[pl.ds(walk.place(at), BLOCK), base : base + width]
        for at in (blk - 1, blk, blk + 1, 0, walk.nblocks - 1)
    ]
    for slot in range(walk.rand):
        halves = []
        for pair in range(heads // 2):
            cols = slice(base + pair * LANES, base + (pair + 1) * LANES)
            first = ref[pl.ds(walk.place(walk.picked(blk, 2 * pair, slot)), BLOCK), cols]
            second = ref[pl.ds(walk.place(walk.picked(blk, 2 * pair + 1, slot)), BLOCK), cols]
            halves.append(jnp.where(left, first, second))
        parts.append(jnp.concatenate(halves, axis=1))
    return jnp.concatenate(parts, axis=0)


def key_marks(mark_ref, walk, blk):
    heads = walk.heads
    left = left_lanes(BLOCK)

    def rows_at(at):
        return mark_ref[pl.ds(pl.multiple_of(at * BLOCK, BLOCK), BLOCK), :]

    before = jnp.where(blk == 1, -1, rows_at(blk - 1))
    after = jnp.where(blk == walk.nblocks - 2, -1, rows_at(blk + 1))
    parts = [
        jnp.concatenate([rows] * (heads // 2), axis=1)
        for rows in (before, rows_at(blk), after, rows_at(0), rows_at(walk.nblocks - 1))
    ]
    for slot in range(walk.rand):
        halves = []
        for pair in range(heads // 2):
            first = rows_at(walk.picked(blk, 2 * pair, slot))
            second = rows_at(walk.picked(blk, 2 * pair + 1, slot))
            halves.append(jnp.where(left, first, second))
        parts.append(jnp.concatenate(halves, axis=1))
    return jnp.concatenate(parts, axis=0)


def chunk_marks(mark_ref, walk, at, size):
    per = walk.nblocks // 4 * BLOCK
    chunk = lax.bitwise_xor(lax.div(at, per), walk.rank)
    natural = pl.multiple_of(chunk * per + lax.rem(at, per), BLOCK)
    rows = mark_ref[pl.ds(natural, size), :]
    return jnp.concatenate([rows] * (walk.heads // 2), axis=1)


def forward_kernel(rank_ref, pick_ref, qkv_ref, mark_ref, qmark_ref, out_ref, score_ref, *, heads, rand, span, near):
    seq = qkv_ref.shape[0]
    width = heads * HEAD_DIM
    walk = Walk(rank_ref, pick_ref, heads, seq, rand)
    first, count, dense = walk.span_of(near)
    base = 0 if near else seq // 2

    def middle(blk):
        place = walk.place(blk)
        query = spread_heads(qkv_ref[pl.ds(place, BLOCK), 0:width], heads)
        keys = gather_rows(qkv_ref, width, walk, blk)
        score = dot_nt(keys, query)
        ok = key_marks(mark_ref, walk, blk) == qmark_ref[pl.ds(blk, 1), :]
        score = jnp.where(ok, score, neg_large)
        expo = jnp.exp(score - jnp.max(score, axis=0, keepdims=True))
        probs = (expo * (1.0 / jnp.sum(expo, axis=0, keepdims=True))).astype(LOW)
        values = gather_rows(qkv_ref, 2 * width, walk, blk)
        out_ref[pl.ds(pl.multiple_of(place - base, BLOCK), BLOCK), :] = own_heads(dot_tn(probs, values), heads).astype(LOW)

    def several(step, carry):
        for k in range(UNROLL_FORWARD):
            middle(first + UNROLL_FORWARD * step + k)
        return carry

    lax.fori_loop(0, count // UNROLL_FORWARD, several, 0)
    for extra in range(count - count % UNROLL_FORWARD, count):
        middle(first + extra)

    place = walk.place(dense)
    query = spread_heads(qkv_ref[pl.ds(place, BLOCK), 0:width], heads)
    qmark = qmark_ref[pl.ds(dense, 1), :]

    def scores_at(step, top):
        at = pl.multiple_of(step * span, span)
        score = dot_nt(qkv_ref[pl.ds(at, span), width : 2 * width], query)
        score = jnp.where(chunk_marks(mark_ref, walk, at, span) == qmark, score, neg_large)
        score_ref[pl.ds(at, span), :] = score
        return jnp.maximum(top, jnp.max(score, axis=0, keepdims=True))

    def expo_at(step, total, top):
        at = pl.multiple_of(step * span, span)
        expo = jnp.exp(score_ref[pl.ds(at, span), :] - top)
        score_ref[pl.ds(at, span), :] = expo
        return total + jnp.sum(expo, axis=0, keepdims=True)

    def value_at(step, total, scale):
        at = pl.multiple_of(step * span, span)
        probs = (score_ref[pl.ds(at, span), :] * scale).astype(LOW)
        return total + dot_tn(probs, qkv_ref[pl.ds(at, span), 2 * width : 3 * width])

    top = jnp.full((1, heads * BLOCK), neg_large, F32)
    top = lax.fori_loop(0, seq // span, scores_at, top)
    total = lax.fori_loop(0, seq // span, partial(expo_at, top=top), jnp.zeros_like(top))
    full = lax.fori_loop(0, seq // span, partial(value_at, scale=1.0 / total), jnp.zeros((heads * BLOCK, width), F32))
    out_ref[pl.ds(pl.multiple_of(place - base, BLOCK), BLOCK), :] = own_heads(full, heads).astype(LOW)


def backward_body(rank_ref, pick_ref, qkv_ref, grad_ref, mark_ref, qmark_ref, query_ref, key_acc, value_acc, score_ref, dprob_ref, heads, rand, span, near):
    seq = qkv_ref.shape[0]
    width = heads * HEAD_DIM
    walk = Walk(rank_ref, pick_ref, heads, seq, rand)
    left = left_lanes(BLOCK)

    first, count, dense = walk.span_of(near)
    base = 0 if near else seq // 2

    def add_rows(acc, rows, blk):
        for index, at in enumerate((blk - 1, blk, blk + 1, 0, walk.nblocks - 1)):
            acc[pl.ds(walk.place(at), BLOCK), :] += rows[index * BLOCK : (index + 1) * BLOCK, :]
        for slot in range(rand):
            row = (5 + slot) * BLOCK
            for pair in range(heads // 2):
                cols = slice(pair * LANES, (pair + 1) * LANES)
                piece = rows[row : row + BLOCK, cols]
                acc[pl.ds(walk.place(walk.picked(blk, 2 * pair, slot)), BLOCK), cols] += jnp.where(left, piece, 0.0)
                acc[pl.ds(walk.place(walk.picked(blk, 2 * pair + 1, slot)), BLOCK), cols] += jnp.where(left, 0.0, piece)

    def middle(blk):
        place = walk.place(blk)
        query = spread_heads(qkv_ref[pl.ds(place, BLOCK), 0:width], heads)
        half_row = pl.multiple_of(place - base, BLOCK)
        grad = spread_heads(grad_ref[pl.ds(half_row, BLOCK), :], heads)
        keys = gather_rows(qkv_ref, width, walk, blk)
        values = gather_rows(qkv_ref, 2 * width, walk, blk)
        score = dot_nt(keys, query)
        ok = key_marks(mark_ref, walk, blk) == qmark_ref[pl.ds(blk, 1), :]
        score = jnp.where(ok, score, neg_large)
        expo = jnp.exp(score - jnp.max(score, axis=0, keepdims=True))
        probs = expo * (1.0 / jnp.sum(expo, axis=0, keepdims=True))
        dprob = dot_nt(values, grad)
        delta = jnp.sum(probs * dprob, axis=0, keepdims=True)
        dscore = (probs * (dprob - delta)).astype(LOW)
        dvalue = dot_nn(probs.astype(LOW), grad)
        dkey = dot_nn(dscore, query)
        dquery = own_heads(dot_tn(dscore, keys), heads)
        query_ref[pl.ds(half_row if near else place, BLOCK), 0:width] = dquery.astype(LOW)
        return dkey, dvalue

    def several(step, carry):
        blk = first + UNROLL * step
        found = [middle(blk + k) for k in range(UNROLL)]
        for k, (dkey, dvalue) in enumerate(found):
            add_rows(key_acc, dkey, blk + k)
            add_rows(value_acc, dvalue, blk + k)
        return carry

    lax.fori_loop(0, count // UNROLL, several, 0)
    for extra in range(count - count % UNROLL, count):
        dkey, dvalue = middle(first + extra)
        add_rows(key_acc, dkey, first + extra)
        add_rows(value_acc, dvalue, first + extra)

    place = walk.place(dense)
    half_row = pl.multiple_of(place - base, BLOCK)
    query = spread_heads(qkv_ref[pl.ds(place, BLOCK), 0:width], heads)
    grad = spread_heads(grad_ref[pl.ds(half_row, BLOCK), :], heads)
    qmark = qmark_ref[pl.ds(dense, 1), :]

    def scores_at(step, top):
        at = pl.multiple_of(step * span, span)
        score = dot_nt(qkv_ref[pl.ds(at, span), width : 2 * width], query)
        score = jnp.where(chunk_marks(mark_ref, walk, at, span) == qmark, score, neg_large)
        score_ref[pl.ds(at, span), :] = score
        dprob_ref[pl.ds(at, span), :] = dot_nt(qkv_ref[pl.ds(at, span), 2 * width : 3 * width], grad)
        return jnp.maximum(top, jnp.max(score, axis=0, keepdims=True))

    def expo_at(step, carry, top):
        total, weighted = carry
        at = pl.multiple_of(step * span, span)
        expo = jnp.exp(score_ref[pl.ds(at, span), :] - top)
        score_ref[pl.ds(at, span), :] = expo
        return (
            total + jnp.sum(expo, axis=0, keepdims=True),
            weighted + jnp.sum(expo * dprob_ref[pl.ds(at, span), :], axis=0, keepdims=True),
        )

    def grads_at(step, dquery, scale, delta):
        at = pl.multiple_of(step * span, span)
        probs = score_ref[pl.ds(at, span), :] * scale
        dscore = (probs * (dprob_ref[pl.ds(at, span), :] - delta)).astype(LOW)
        value_acc[pl.ds(at, span), :] += dot_nn(probs.astype(LOW), grad)
        key_acc[pl.ds(at, span), :] += dot_nn(dscore, query)
        return dquery + dot_tn(dscore, qkv_ref[pl.ds(at, span), width : 2 * width])

    top = jnp.full((1, heads * BLOCK), neg_large, F32)
    top = lax.fori_loop(0, seq // span, scores_at, top)
    total, weighted = lax.fori_loop(0, seq // span, partial(expo_at, top=top), (jnp.zeros_like(top), jnp.zeros_like(top)))
    scale = 1.0 / total
    full = lax.fori_loop(0, seq // span, partial(grads_at, scale=scale, delta=weighted * scale), jnp.zeros((heads * BLOCK, width), F32))
    query_ref[pl.ds(half_row if near else place, BLOCK), 0:width] = own_heads(full, heads).astype(LOW)


def backward_near(rank_ref, pick_ref, qkv_ref, grad_ref, mark_ref, qmark_ref, query_ref, key_acc, value_acc, score_ref, dprob_ref, *, heads, rand, span):
    seq = qkv_ref.shape[0]
    width = heads * HEAD_DIM

    def clear(step, carry):
        at = pl.multiple_of(step * span, span)
        key_acc[pl.ds(at, span), :] = jnp.zeros((span, width), F32)
        value_acc[pl.ds(at, span), :] = jnp.zeros((span, width), F32)
        return carry

    lax.fori_loop(0, seq // span, clear, 0)
    backward_body(rank_ref, pick_ref, qkv_ref, grad_ref, mark_ref, qmark_ref, query_ref, key_acc, value_acc, score_ref, dprob_ref, heads, rand, span, True)


def backward_far(rank_ref, pick_ref, qkv_ref, grad_ref, mark_ref, qmark_ref, near_ref, key_in, value_in, out_ref, key_acc, value_acc, score_ref, dprob_ref, *, heads, rand, span):
    seq = qkv_ref.shape[0]
    width = heads * HEAD_DIM

    def begin(step, carry):
        at = pl.multiple_of(step * span, span)
        key_acc[pl.ds(at, span), :] = key_in[pl.ds(at, span), :]
        value_acc[pl.ds(at, span), :] = value_in[pl.ds(at, span), :]
        return carry

    lax.fori_loop(0, seq // span, begin, 0)
    out_ref[0 : seq // 2, 0:width] = near_ref[...]
    backward_body(rank_ref, pick_ref, qkv_ref, grad_ref, mark_ref, qmark_ref, out_ref, key_acc, value_acc, score_ref, dprob_ref, heads, rand, span, False)

    def finish(step, carry):
        at = pl.multiple_of(step * span, span)
        out_ref[pl.ds(at, span), width : 2 * width] = key_acc[pl.ds(at, span), :].astype(LOW)
        out_ref[pl.ds(at, span), 2 * width : 3 * width] = value_acc[pl.ds(at, span), :].astype(LOW)
        return carry

    lax.fori_loop(0, seq // span, finish, 0)


def token_marks(seq_segs, heads):
    seq = seq_segs.shape[0]
    marks = jnp.where(seq_segs != 0, seq_segs, 1000 + jnp.arange(seq, dtype=jnp.int32))
    by_row = jnp.broadcast_to(marks[:, None], (seq, LANES))
    by_block = jnp.tile(marks.reshape(seq // BLOCK, BLOCK), (1, heads))
    return by_row, by_block


def spent(micros):
    return pl.CostEstimate(flops=micros * 10**9, bytes_accessed=micros * 10**6, transcendentals=0)


SMEM_SPEC = pl.BlockSpec(memory_space=pltpu.SMEM)
VMEM_SPEC = pl.BlockSpec(memory_space=pltpu.VMEM)


def attend(rank, picks, qkv, marks, near):
    heads, _, rand = picks.shape
    seq = qkv.shape[0]
    width = heads * HEAD_DIM
    span = min(512, seq // 4)
    return pl.pallas_call(
        partial(forward_kernel, heads=heads, rand=rand, span=span, near=near),
        out_shape=jax.ShapeDtypeStruct((seq // 2, width), LOW),
        in_specs=[SMEM_SPEC, SMEM_SPEC, VMEM_SPEC, VMEM_SPEC, VMEM_SPEC],
        out_specs=VMEM_SPEC,
        scratch_shapes=[pltpu.VMEM((seq, heads * BLOCK), F32)],
        name="attend_near" if near else "attend_far",
        cost_estimate=spent(1),
    )(rank, picks.reshape(-1), qkv, *marks)


def attend_back_near(rank, picks, qkv, grad_context, marks):
    heads, _, rand = picks.shape
    seq = qkv.shape[0]
    width = heads * HEAD_DIM
    span = min(512, seq // 4)
    total = jax.ShapeDtypeStruct((seq, width), F32)
    return pl.pallas_call(
        partial(backward_near, heads=heads, rand=rand, span=span),
        out_shape=[jax.ShapeDtypeStruct((seq // 2, width), LOW), total, total],
        in_specs=[SMEM_SPEC, SMEM_SPEC, VMEM_SPEC, VMEM_SPEC, VMEM_SPEC, VMEM_SPEC],
        out_specs=[VMEM_SPEC] * 3,
        scratch_shapes=[pltpu.VMEM((seq, heads * BLOCK), F32)] * 2,
        name="attend_back_near",
        cost_estimate=spent(40),
    )(rank, picks.reshape(-1), qkv, grad_context, *marks)


def attend_back_far(rank, picks, qkv, grad_context, marks, near_parts):
    heads, _, rand = picks.shape
    seq = qkv.shape[0]
    width = heads * HEAD_DIM
    span = min(512, seq // 4)
    return pl.pallas_call(
        partial(backward_far, heads=heads, rand=rand, span=span),
        out_shape=jax.ShapeDtypeStruct((seq, 3 * width), LOW),
        in_specs=[SMEM_SPEC, SMEM_SPEC] + [VMEM_SPEC] * 7,
        out_specs=VMEM_SPEC,
        scratch_shapes=[pltpu.VMEM((seq, width), F32)] * 2 + [pltpu.VMEM((seq, heads * BLOCK), F32)] * 2,
        name="attend_back_far",
        cost_estimate=spent(43),
    )(rank, picks.reshape(-1), qkv, grad_context, *marks, *near_parts)


eps_norm = 1e-05


def by_rows(values):
    return with_layout_constraint(values, Layout(major_to_minor=(0, 1)))


def tie(values, *others):
    return lax.optimization_barrier((values, others))[0]


def norm_rows(source, gain_vec, shift_vec):
    average = jnp.mean(source, axis=-1, keepdims=True)
    centred = source - average
    variance = jnp.mean(centred * centred, axis=-1, keepdims=True)
    return centred * lax.rsqrt(variance + eps_norm) * gain_vec + shift_vec


def norm_kernel(source_ref, gain_ref, shift_ref, out_ref):
    source = source_ref[...].astype(F32)
    out_ref[...] = norm_rows(source, gain_ref[...], shift_ref[...]).astype(LOW)


def norm_call(source, gain, shift):
    rows, model = source.shape
    tile = min(512, rows)
    vector = pl.BlockSpec((1, model), lambda i: (0, 0))
    block = pl.BlockSpec((tile, model), lambda i: (i, 0))
    return pl.pallas_call(
        norm_kernel,
        grid=(rows // tile,),
        in_specs=[block, vector, vector],
        out_specs=block,
        out_shape=jax.ShapeDtypeStruct((rows, model), LOW),
        name="norm",
        cost_estimate=spent(3),
    )(source, gain, shift)


def norm_back_kernel(source_ref, gain_ref, residual_ref, *rest, terms, narrow):
    term_refs = rest[:terms]
    out_ref = rest[terms]
    low_ref = rest[terms + 1] if narrow else None
    sum_ref = rest[-1]
    source = source_ref[...].astype(F32)
    grad = term_refs[0][...].astype(F32)
    for ref in term_refs[1:]:
        grad = grad + ref[...].astype(F32)
    average = jnp.mean(source, axis=-1, keepdims=True)
    centred = source - average
    variance = jnp.mean(centred * centred, axis=-1, keepdims=True)
    scale = lax.rsqrt(variance + eps_norm)
    normal = centred * scale
    scaled = grad * gain_ref[...]
    first = jnp.mean(scaled, axis=-1, keepdims=True)
    second = jnp.mean(scaled * normal, axis=-1, keepdims=True)
    residual = residual_ref[...].astype(F32)
    full = residual + scale * (scaled - first - normal * second)
    out_ref[...] = full
    if narrow:
        low_ref[...] = full.astype(LOW)
    model = source.shape[1]
    parts = [jnp.sum(grad * normal, axis=0, keepdims=True), jnp.sum(grad, axis=0, keepdims=True)]
    if narrow:
        parts.append(jnp.sum(residual, axis=0, keepdims=True))
    parts.append(jnp.zeros((8 - len(parts), model), F32))
    parts = jnp.concatenate(parts, axis=0)

    @pl.when(pl.program_id(0) == 0)
    def _():
        sum_ref[...] = parts

    @pl.when(pl.program_id(0) != 0)
    def _():
        sum_ref[...] += parts


def norm_back(source, gain, residual, terms, narrow):
    rows, model = source.shape
    tile = min(512, rows)
    vector = pl.BlockSpec((1, model), lambda i: (0, 0))
    block = pl.BlockSpec((tile, model), lambda i: (i, 0))
    shapes = [jax.ShapeDtypeStruct((rows, model), F32)]
    if narrow:
        shapes.append(jax.ShapeDtypeStruct((rows, model), LOW))
    return pl.pallas_call(
        partial(norm_back_kernel, terms=len(terms), narrow=narrow),
        grid=(rows // tile,),
        in_specs=[block, vector] + [block] * (1 + len(terms)),
        out_specs=[block] * len(shapes) + [pl.BlockSpec((8, model), lambda i: (0, 0))],
        out_shape=shapes + [jax.ShapeDtypeStruct((8, model), F32)],
        name="norm_back",
        cost_estimate=spent(7),
    )(source, gain, residual, *terms)


def down_kernel(hidden_ref, part_ref, down_ref, side_ref, own_ref, *, step):
    def run(out_ref):
        for at in range(0, hidden_ref.shape[0], step):
            rows = slice(at, at + step)
            out_ref[rows, :] = (part_ref[rows, :] + dot_nt(hidden_ref[rows, :], down_ref[...])).astype(out_ref.dtype)

    @pl.when(pl.program_id(0) == 0)
    def _():
        run(side_ref)

    @pl.when(pl.program_id(0) == 1)
    def _():
        run(own_ref)


def down_call(hidden, part, weights):
    rows = hidden.shape[0] // 2
    units = hidden.shape[1]
    model = weights.shape[0]
    last = weights.shape[1] // units - 1
    out = pl.BlockSpec((rows, model), lambda t: (0, 0))
    return pl.pallas_call(
        partial(down_kernel, step=min(512, rows)),
        grid=(2,),
        in_specs=[
            pl.BlockSpec((rows, units), lambda t: (1 - t, 0)),
            pl.BlockSpec((rows, model), lambda t: (1 - t, 0)),
            pl.BlockSpec((model, units), lambda t: (0, last)),
        ],
        out_specs=[out, out],
        out_shape=[jax.ShapeDtypeStruct((rows, model), LOW), jax.ShapeDtypeStruct((rows, model), F32)],
        name="down",
        cost_estimate=spent(1),
    )(hidden, part, weights)


def finish_kernel(middle_ref, own_ref, back_ref, bias_ref, valid_ref, out_ref, sum_ref):
    branch = own_ref[...] + back_ref[...].astype(F32) + bias_ref[...]
    out_ref[...] = (middle_ref[...] + branch).astype(LOW)
    squares = jnp.sum(valid_ref[...] * branch * branch, axis=0, keepdims=True)

    @pl.when(pl.program_id(0) == 0)
    def _():
        sum_ref[...] = squares

    @pl.when(pl.program_id(0) != 0)
    def _():
        sum_ref[...] += squares


def finish_call(middle, own, back, bias, valid):
    rows, model = middle.shape
    tile = min(512, rows)
    vector = pl.BlockSpec((1, model), lambda i: (0, 0))
    block = pl.BlockSpec((tile, model), lambda i: (i, 0))
    return pl.pallas_call(
        finish_kernel,
        grid=(rows // tile,),
        in_specs=[block, block, block, vector, pl.BlockSpec((tile, 1), lambda i: (i, 0))],
        out_specs=[block, vector],
        out_shape=[jax.ShapeDtypeStruct((rows, model), LOW), jax.ShapeDtypeStruct((1, model), F32)],
        name="finish",
        cost_estimate=spent(1),
    )(middle, own, back, bias, valid)


def feed_kernel(second_own, second_side, grad_own, grad_side, up_ref, down_ref, bias_ref, hidden_ref, pre_ref, sum_ref, *, step):
    slope = (2.0 / jnp.pi) ** 0.5

    def run(second_ref, grad_ref):
        total = jnp.zeros(sum_ref.shape[1:], F32)
        for at in range(0, second_ref.shape[0], step):
            rows = slice(at, at + step)
            unit = dot_nn(second_ref[rows, :], up_ref[...]) + bias_ref[...]
            grad = dot_nn(grad_ref[rows, :], down_ref[...])
            square = unit * unit
            bent = jnp.tanh(unit * (slope + (slope * 0.044715) * square))
            half = 0.5 + 0.5 * bent
            hidden_ref[rows, :] = (unit * half).astype(LOW)
            rise = half + (0.5 * unit) * (1.0 - bent * bent) * (slope + (slope * 0.134145) * square)
            low = (grad * rise).astype(LOW)
            pre_ref[rows, :] = low
            total = total + jnp.sum(low.astype(F32), axis=0, keepdims=True)
        sum_ref[0] = total

    @pl.when(pl.program_id(0) == 0)
    def _():
        run(second_own, grad_own)

    @pl.when(pl.program_id(0) == 1)
    def _():
        run(second_side, grad_side)


def feed(seconds, grads, weights, first_up, first_down, bias):
    rows, model = seconds[0].shape
    units = bias.shape[0]
    tile = min(512, units)
    whole = pl.BlockSpec((rows, model), lambda t, u: (0, 0))
    out = pl.BlockSpec((rows, tile), lambda t, u: (t, u))
    return pl.pallas_call(
        partial(feed_kernel, step=min(128, rows)),
        grid=(2, units // tile),
        in_specs=[whole] * 4
        + [
            pl.BlockSpec((model, tile), lambda t, u: (0, first_up // tile + u)),
            pl.BlockSpec((model, tile), lambda t, u: (0, first_down // tile + u)),
            pl.BlockSpec((1, tile), lambda t, u: (0, u)),
        ],
        out_specs=[out, out, pl.BlockSpec((1, 1, tile), lambda t, u: (t, 0, u))],
        out_shape=[
            jax.ShapeDtypeStruct((2 * rows, units), LOW),
            jax.ShapeDtypeStruct((2 * rows, units), LOW),
            jax.ShapeDtypeStruct((2, 1, units), F32),
        ],
        name="feed",
        cost_estimate=spent(3),
    )(*seconds, *grads, weights, weights, bias[None])


def swap(values, axis, mask):
    count = lax.axis_size(axis)
    return lax.ppermute(values, axis, [(i, i ^ mask) for i in range(count)])


def collect_rows(parts, *hooks):
    hooks = list(hooks)
    count = lax.axis_size("fsdp")
    spot = lax.axis_index("fsdp")
    rows = parts[0].shape[0] // count
    mask = 1
    while mask < count:
        upper = (spot & mask) != 0
        parts = [part.reshape(-1, 2, rows, part.shape[-1]) for part in parts]
        sent = [jnp.where(upper, part[:, 0], part[:, 1]).astype(LOW) for part in parts]
        got = swap(jnp.concatenate(sent, -1), "fsdp", mask)
        first = 0
        held = []
        for part in parts:
            last = first + part.shape[-1]
            held.append(jnp.where(upper, part[:, 1], part[:, 0]) + got[..., first:last].astype(F32))
            first = last
        parts = hooks.pop(0)(held) if hooks else held
        mask *= 2
    return [part.reshape(rows, part.shape[-1]) for part in parts]


def total_over(values, axis):
    bits = [1 << k for k in range(lax.axis_size(axis).bit_length() - 1)]
    while bits:
        if len(bits) % 2:
            values = values + swap(values, axis, bits.pop(0))
        else:
            low, high = bits.pop(0), bits.pop(0)
            values = (values + swap(values, axis, low)) + (swap(values, axis, high) + swap(values, axis, low | high))
    return values


def on_device(
    hidden_in,
    cotangent,
    norm1_gain,
    norm1_bias,
    w_query,
    w_key,
    w_value,
    w_out,
    norm2_gain,
    norm2_bias,
    w_fc1,
    bias_fc1,
    w_fc2,
    bias_fc2,
    segments,
    random_blocks,
):
    rows_dev, width_model = hidden_in.shape
    heads_wide = w_query.shape[1]
    rank = lax.axis_index("tp")
    seq_segs = segments[0]
    picks = random_blocks[0]
    heads_local = picks.shape[0]
    own_segs = lax.dynamic_slice_in_dim(seq_segs, rank * rows_dev, rows_dev)
    valid_rows = (own_segs != 0).astype(F32)[:, None]
    gain_first = norm1_gain.astype(F32)[None]
    shift_first = norm1_bias.astype(F32)[None]
    gain_second = norm2_gain.astype(F32)[None]
    shift_second = norm2_bias.astype(F32)[None]
    residual_in = hidden_in.astype(F32)
    scale_query = HEAD_DIM ** (-0.5)
    rank_word = rank.astype(jnp.int32).reshape(1)
    marks = token_marks(seq_segs, heads_local)

    heads_local_w = by_rows(jnp.concatenate([w_query * jnp.asarray(scale_query, LOW), w_key, w_value, w_out.T], 1))
    w_heads = lax.all_gather(heads_local_w, "fsdp", axis=0, tiled=True)
    pair_local = by_rows(jnp.concatenate([w_fc1, w_fc2.T], 1))
    units = w_fc1.shape[1]
    own_all = lax.all_gather(pair_local, "fsdp", axis=0, tiled=True)
    far_hidden = swap(hidden_in, "tp", 2)
    far_local = swap(tie(pair_local, far_hidden), "tp", 2)
    bias_up = [bias_fc1.astype(F32), swap(bias_fc1, "tp", 2).astype(F32)]

    first_own = norm_call(tie(hidden_in, marks, picks), gain_first, shift_first)
    first_side = swap(first_own, "tp", 1)
    far_hidden, w_heads = lax.optimization_barrier((far_hidden, w_heads))
    w_qkv = w_heads[:, : 3 * heads_wide]
    first_far = norm_call(far_hidden, gain_first, shift_first)
    first_cross = swap(first_far, "tp", 1)
    chunks = (first_own, first_side, first_far, first_cross)
    qkv = jnp.concatenate([dot_nn(chunk, w_qkv).astype(LOW) for chunk in chunks], 0)
    qkv, far_local = lax.optimization_barrier((qkv, far_local))
    far_all = lax.all_gather(far_local, "fsdp", axis=0, tiled=True)
    context_far = attend(rank_word, picks, qkv, marks, False)
    context_cross = [swap(context_far[k * rows_dev : (k + 1) * rows_dev], "tp", 2 + k) for k in (0, 1)]
    wo_own = tie(w_heads, qkv)[:, 3 * heads_wide :]
    wo_pair = jnp.concatenate([wo_own, swap(wo_own, "tp", 2)], 1)
    wo_side = swap(wo_pair, "tp", 1)
    wo_all = by_rows(jnp.concatenate(
        [wo_pair[:, :heads_wide], wo_side[:, :heads_wide], wo_pair[:, heads_wide:], wo_side[:, heads_wide:]], 1
    ))
    context_near = attend(rank_word, picks, tie(qkv, context_far), marks, True)
    side_context, context_cross = lax.optimization_barrier((context_near[rows_dev:], context_cross))
    context_cat = by_rows(jnp.concatenate(
        [context_near[:rows_dev], swap(side_context, "tp", 1)] + context_cross, 1
    ))
    attn_branch = by_rows(dot_nt(context_cat, wo_all))
    middle = residual_in + attn_branch
    early_rows = jnp.concatenate(
        [jnp.full((1, width_model), jnp.sum(valid_rows))]
        + [
            jnp.sum(valid_rows * branch * branch, axis=0, keepdims=True)
            for branch in (residual_in, attn_branch, middle)
        ]
    )
    second_own = by_rows(norm_rows(middle, gain_second, shift_second).astype(LOW))

    second_side = swap(second_own, "tp", 1)
    grad_side = swap(cotangent, "tp", 1)
    tokens = (second_own, second_side), (cotangent, grad_side)
    first = feed(*tokens, own_all, 0, units, bias_up[0])
    down_part = by_rows(dot_nt(first[0], own_all[:, units:]))
    up_part = by_rows(dot_nt(first[1], own_all[:, :units]))
    far_all, down_part, up_part = lax.optimization_barrier((far_all, down_part, up_part))
    hidden, grad_pre, bias_parts = zip(first, feed(*tokens, far_all, 0, units, bias_up[1]))
    w_up_far = far_all[:, :units]
    side_terms = up_part[rows_dev:] + dot_nt(grad_pre[1][rows_dev:], w_up_far)
    side_back = swap(by_rows(side_terms.astype(LOW)), "tp", 1)
    own_terms = up_part[:rows_dev] + dot_nt(grad_pre[1][:rows_dev], w_up_far)
    second_two = jnp.concatenate([second_own, second_side], 0)
    grad_two = jnp.concatenate([cotangent, grad_side], 0)
    share = by_rows(jnp.concatenate(
        [dot_tn(second_two, grad_pre[half]).astype(LOW) for half in range(2)]
        + [dot_tn(grad_two, hidden[half]).astype(LOW) for half in range(2)],
        1,
    ))
    grad_middle, grad_attn, second_sums = norm_back(middle, gain_second, cotangent, (by_rows(own_terms), side_back), True)

    grad_context_cat = dot_nn(grad_attn, wo_all).astype(LOW)
    grad_parts = [grad_context_cat[:, k * heads_wide : (k + 1) * heads_wide] for k in range(4)]
    grad_far = jnp.concatenate([swap(grad_parts[2], "tp", 2), swap(grad_parts[3], "tp", 3)], 0)
    grad_near = jnp.concatenate([grad_parts[0], swap(grad_parts[1], "tp", 1)], 0)
    out_terms = by_rows(dot_tn(grad_attn, context_cat))
    out_near = [out_terms[:, k * heads_wide : (k + 1) * heads_wide] for k in range(4)]
    out_chip = [
        out_near[k] + swap(out_near[k + 1].astype(LOW), "tp", 1).astype(F32) for k in (0, 2)
    ]
    out_sum = out_chip[0] + swap(out_chip[1].astype(LOW), "tp", 2).astype(F32)
    grad_near, share, out_terms = lax.optimization_barrier((grad_near, share, out_terms))
    share = lax.psum_scatter(share, "fsdp", scatter_dimension=0, tiled=True)
    near_parts = attend_back_near(rank_word, picks, qkv, grad_near, marks)
    bias_terms = [jnp.sum(parts, axis=0) for parts in bias_parts]
    grad_bias_up = bias_terms[0] + swap(bias_terms[1], "tp", 2)
    out_sum, grad_far, near_parts, grad_bias_up = lax.optimization_barrier(
        (out_sum, grad_far, near_parts, grad_bias_up)
    )
    grad_qkv = attend_back_far(rank_word, picks, qkv, grad_far, marks, near_parts)
    far_side = by_rows(dot_nt(grad_qkv[3 * rows_dev :], w_qkv).astype(LOW))
    far_own = by_rows(dot_nt(grad_qkv[2 * rows_dev : 3 * rows_dev], w_qkv))
    far_side, far_own = lax.optimization_barrier((swap(far_side, "tp", 1), far_own))
    far_low = (far_own + far_side.astype(F32)).astype(LOW)
    far_back = swap(far_low, "tp", 2)

    grad_qkv_late = tie(grad_qkv, far_low)
    qkv_terms = by_rows(dot_tn(jnp.concatenate(chunks, 0), grad_qkv_late))
    hidden_far, grad_qkv_late = tie((hidden[1], grad_qkv_late), qkv_terms)
    near_side = by_rows(dot_nt(grad_qkv_late[rows_dev : 2 * rows_dev], w_qkv).astype(LOW))
    near_own = by_rows(dot_nt(grad_qkv_late[:rows_dev], w_qkv))
    near_back = swap(near_side, "tp", 1)
    down_side, down_own = down_call(hidden_far, down_part, far_all)
    output_rows, branch_squares = finish_call(
        middle, down_own, swap(down_side, "tp", 1), bias_fc2.astype(F32)[None], valid_rows
    )
    square_rows = jnp.concatenate([early_rows, branch_squares])

    gathered = {}

    def after_first(parts):
        parts, (back, rows_out, squares, part, near) = lax.optimization_barrier(
            (parts, (far_back, output_rows, square_rows, share, near_back))
        )
        part = part.astype(F32)
        cross = jnp.concatenate([part[:, units : 2 * units], part[:, 3 * units :]], 1)
        cross = swap(cross.astype(LOW), "tp", 2)
        grad_in, sums_in = norm_back(hidden_in, gain_first, grad_middle, (near_own, near, back), False)
        gathered.update(share=part, across=cross, output=rows_out, squares=squares, input=grad_in, sums=sums_in)
        return parts

    def after_second(parts):
        parts, gathered["sums"], gathered["across"] = lax.optimization_barrier(
            (parts, gathered["sums"], gathered["across"])
        )
        return parts

    collected, grad_w_o = collect_rows([qkv_terms, out_sum], after_first, after_second)
    share, across, first_sums = gathered["share"], gathered["across"], gathered["sums"]
    output_rows, square_rows, grad_input = gathered["output"], gathered["squares"], gathered["input"]
    across = across.astype(F32)
    grad_w_up = share[:, :units] + across[:, :units]
    grad_w_down = (share[:, 2 * units : 3 * units] + across[:, units:]).T
    grad_w_q = collected[:, :heads_wide] * scale_query
    grad_w_k = collected[:, heads_wide : 2 * heads_wide]
    grad_w_v = collected[:, 2 * heads_wide :]
    grad_w_o = grad_w_o.T

    sums = jnp.concatenate([second_sums[:3], square_rows, first_sums[:2]])
    sums = total_over(sums, "tp")
    bias_rows = grad_bias_up.reshape(-1, width_model)
    sums = total_over(jnp.concatenate([sums, bias_rows]), "fsdp")
    residual_rms = jnp.sqrt(jnp.sum(sums[4:8], axis=1) / (sums[3, 0] * width_model))
    return (
        output_rows,
        grad_input,
        sums[8],
        sums[9],
        grad_w_q,
        grad_w_k,
        grad_w_v,
        grad_w_o,
        sums[0],
        sums[1],
        grad_w_up,
        sums[10:].reshape(-1),
        grad_w_down,
        sums[2],
        residual_rms,
    )


def solution(mesh):
    in_specs = (
        P(("fsdp", "tp"), None),
        P(("fsdp", "tp"), None),
        P(),
        P(),
        P("fsdp", "tp"),
        P("fsdp", "tp"),
        P("fsdp", "tp"),
        P("tp", "fsdp"),
        P(),
        P(),
        P("fsdp", "tp"),
        P("tp"),
        P("tp", "fsdp"),
        P(),
        P("fsdp", None),
        P("fsdp", "tp", None, None),
    )
    out_specs = (
        P(("fsdp", "tp"), None),
        P(("fsdp", "tp"), None),
        P(),
        P(),
        P("fsdp", "tp"),
        P("fsdp", "tp"),
        P("fsdp", "tp"),
        P("tp", "fsdp"),
        P(),
        P(),
        P("fsdp", "tp"),
        P("tp"),
        P("tp", "fsdp"),
        P(),
        P(),
    )
    return jax.shard_map(
        on_device, mesh=mesh, in_specs=in_specs, out_specs=out_specs, check_vma=False
    )
```

```python
from functools import partial
import jax, jax.numpy as jnp
from jax import lax
from jax.experimental import pallas as pl
from jax.experimental.layout import Layout, with_layout_constraint
from jax.experimental.pallas import tpu as pltpu
from jax.sharding import PartitionSpec as P

HEAD_DIM = 64
BLOCK = 64
LANES = 128
F32 = jnp.float32
LOW = jnp.bfloat16
neg_large = -1e30
UNROLL = 5
UNROLL_FORWARD = 10


def dot_nn(a, b):
    return lax.dot_general(a, b, (((1,), (0,)), ((), ())), preferred_element_type=F32)


def dot_nt(a, b):
    return lax.dot_general(a, b, (((1,), (1,)), ((), ())), preferred_element_type=F32)


def dot_tn(a, b):
    return lax.dot_general(a, b, (((0,), (0,)), ((), ())), preferred_element_type=F32)


class Walk:
    def __init__(self, rank_ref, pick_ref, heads, seq, rand):
        self.rank = rank_ref[0]
        self.pick_ref = pick_ref
        self.heads = heads
        self.rand = rand
        self.nblocks = seq // BLOCK

    def place(self, blk):
        per = self.nblocks // 4
        chunk = lax.bitwise_xor(lax.div(blk, per), self.rank)
        return pl.multiple_of((chunk * per + lax.rem(blk, per)) * BLOCK, BLOCK)

    def span_of(self, near):
        upper = lax.div(self.rank, 2)
        half = upper if near else 1 - upper
        count = self.nblocks // 2 - 1
        return 1 + half * count, count, half * (self.nblocks - 1)

    def picked(self, blk, head, slot):
        return self.pick_ref[(head * (self.nblocks - 2) + blk - 1) * self.rand + slot]


def left_lanes(rows):
    return lax.broadcasted_iota(jnp.int32, (rows, LANES), 1) < HEAD_DIM


def spread_heads(rows, heads):
    tall = jnp.concatenate([rows.astype(F32)] * heads, axis=0)
    width = heads * HEAD_DIM
    row_head = lax.broadcasted_iota(jnp.int32, (heads * BLOCK, width), 0) // BLOCK
    col_head = lax.broadcasted_iota(jnp.int32, (heads * BLOCK, width), 1) // HEAD_DIM
    return jnp.where(row_head == col_head, tall, 0.0).astype(LOW)


def own_heads(full, heads):
    left = left_lanes(BLOCK)
    halves = []
    for pair in range(heads // 2):
        cols = slice(pair * LANES, (pair + 1) * LANES)
        first = full[2 * pair * BLOCK : (2 * pair + 1) * BLOCK, cols]
        second = full[(2 * pair + 1) * BLOCK : (2 * pair + 2) * BLOCK, cols]
        halves.append(jnp.where(left, first, second))
    return jnp.concatenate(halves, axis=1)


def gather_rows(ref, base, walk, blk):
    heads = walk.heads
    width = heads * HEAD_DIM
    left = left_lanes(BLOCK)
    parts = [
        ref[pl.ds(walk.place(at), BLOCK), base : base + width]
        for at in (blk - 1, blk, blk + 1, 0, walk.nblocks - 1)
    ]
    for slot in range(walk.rand):
        halves = []
        for pair in range(heads // 2):
            cols = slice(base + pair * LANES, base + (pair + 1) * LANES)
            first = ref[pl.ds(walk.place(walk.picked(blk, 2 * pair, slot)), BLOCK), cols]
            second = ref[pl.ds(walk.place(walk.picked(blk, 2 * pair + 1, slot)), BLOCK), cols]
            halves.append(jnp.where(left, first, second))
        parts.append(jnp.concatenate(halves, axis=1))
    return jnp.concatenate(parts, axis=0)


def key_marks(mark_ref, walk, blk):
    heads = walk.heads
    left = left_lanes(BLOCK)

    def rows_at(at):
        return mark_ref[pl.ds(pl.multiple_of(at * BLOCK, BLOCK), BLOCK), :]

    before = jnp.where(blk == 1, -1, rows_at(blk - 1))
    after = jnp.where(blk == walk.nblocks - 2, -1, rows_at(blk + 1))
    parts = [
        jnp.concatenate([rows] * (heads // 2), axis=1)
        for rows in (before, rows_at(blk), after, rows_at(0), rows_at(walk.nblocks - 1))
    ]
    for slot in range(walk.rand):
        halves = []
        for pair in range(heads // 2):
            first = rows_at(walk.picked(blk, 2 * pair, slot))
            second = rows_at(walk.picked(blk, 2 * pair + 1, slot))
            halves.append(jnp.where(left, first, second))
        parts.append(jnp.concatenate(halves, axis=1))
    return jnp.concatenate(parts, axis=0)


def chunk_marks(mark_ref, walk, at, size):
    per = walk.nblocks // 4 * BLOCK
    chunk = lax.bitwise_xor(lax.div(at, per), walk.rank)
    natural = pl.multiple_of(chunk * per + lax.rem(at, per), BLOCK)
    rows = mark_ref[pl.ds(natural, size), :]
    return jnp.concatenate([rows] * (walk.heads // 2), axis=1)


def forward_kernel(rank_ref, pick_ref, qkv_ref, mark_ref, qmark_ref, out_ref, score_ref, *, heads, rand, span, near):
    seq = qkv_ref.shape[0]
    width = heads * HEAD_DIM
    walk = Walk(rank_ref, pick_ref, heads, seq, rand)
    first, count, dense = walk.span_of(near)
    base = 0 if near else seq // 2

    def middle(blk):
        place = walk.place(blk)
        query = spread_heads(qkv_ref[pl.ds(place, BLOCK), 0:width], heads)
        keys = gather_rows(qkv_ref, width, walk, blk)
        score = dot_nt(keys, query)
        ok = key_marks(mark_ref, walk, blk) == qmark_ref[pl.ds(blk, 1), :]
        score = jnp.where(ok, score, neg_large)
        expo = jnp.exp(score - jnp.max(score, axis=0, keepdims=True))
        probs = (expo * (1.0 / jnp.sum(expo, axis=0, keepdims=True))).astype(LOW)
        values = gather_rows(qkv_ref, 2 * width, walk, blk)
        out_ref[pl.ds(pl.multiple_of(place - base, BLOCK), BLOCK), :] = own_heads(dot_tn(probs, values), heads).astype(LOW)

    def several(step, carry):
        for k in range(UNROLL_FORWARD):
            middle(first + UNROLL_FORWARD * step + k)
        return carry

    lax.fori_loop(0, count // UNROLL_FORWARD, several, 0)
    for extra in range(count - count % UNROLL_FORWARD, count):
        middle(first + extra)

    place = walk.place(dense)
    query = spread_heads(qkv_ref[pl.ds(place, BLOCK), 0:width], heads)
    qmark = qmark_ref[pl.ds(dense, 1), :]

    def scores_at(step, top):
        at = pl.multiple_of(step * span, span)
        score = dot_nt(qkv_ref[pl.ds(at, span), width : 2 * width], query)
        score = jnp.where(chunk_marks(mark_ref, walk, at, span) == qmark, score, neg_large)
        score_ref[pl.ds(at, span), :] = score
        return jnp.maximum(top, jnp.max(score, axis=0, keepdims=True))

    def expo_at(step, total, top):
        at = pl.multiple_of(step * span, span)
        expo = jnp.exp(score_ref[pl.ds(at, span), :] - top)
        score_ref[pl.ds(at, span), :] = expo
        return total + jnp.sum(expo, axis=0, keepdims=True)

    def value_at(step, total, scale):
        at = pl.multiple_of(step * span, span)
        probs = (score_ref[pl.ds(at, span), :] * scale).astype(LOW)
        return total + dot_tn(probs, qkv_ref[pl.ds(at, span), 2 * width : 3 * width])

    top = jnp.full((1, heads * BLOCK), neg_large, F32)
    top = lax.fori_loop(0, seq // span, scores_at, top)
    total = lax.fori_loop(0, seq // span, partial(expo_at, top=top), jnp.zeros_like(top))
    full = lax.fori_loop(0, seq // span, partial(value_at, scale=1.0 / total), jnp.zeros((heads * BLOCK, width), F32))
    out_ref[pl.ds(pl.multiple_of(place - base, BLOCK), BLOCK), :] = own_heads(full, heads).astype(LOW)


def backward_body(rank_ref, pick_ref, qkv_ref, grad_ref, mark_ref, qmark_ref, query_ref, key_acc, value_acc, score_ref, dprob_ref, heads, rand, span, near):
    seq = qkv_ref.shape[0]
    width = heads * HEAD_DIM
    walk = Walk(rank_ref, pick_ref, heads, seq, rand)
    left = left_lanes(BLOCK)

    first, count, dense = walk.span_of(near)
    base = 0 if near else seq // 2

    def add_rows(acc, rows, blk):
        for index, at in enumerate((blk - 1, blk, blk + 1, 0, walk.nblocks - 1)):
            acc[pl.ds(walk.place(at), BLOCK), :] += rows[index * BLOCK : (index + 1) * BLOCK, :]
        for slot in range(rand):
            row = (5 + slot) * BLOCK
            for pair in range(heads // 2):
                cols = slice(pair * LANES, (pair + 1) * LANES)
                piece = rows[row : row + BLOCK, cols]
                acc[pl.ds(walk.place(walk.picked(blk, 2 * pair, slot)), BLOCK), cols] += jnp.where(left, piece, 0.0)
                acc[pl.ds(walk.place(walk.picked(blk, 2 * pair + 1, slot)), BLOCK), cols] += jnp.where(left, 0.0, piece)

    def middle(blk):
        place = walk.place(blk)
        query = spread_heads(qkv_ref[pl.ds(place, BLOCK), 0:width], heads)
        half_row = pl.multiple_of(place - base, BLOCK)
        grad = spread_heads(grad_ref[pl.ds(half_row, BLOCK), :], heads)
        keys = gather_rows(qkv_ref, width, walk, blk)
        values = gather_rows(qkv_ref, 2 * width, walk, blk)
        score = dot_nt(keys, query)
        ok = key_marks(mark_ref, walk, blk) == qmark_ref[pl.ds(blk, 1), :]
        score = jnp.where(ok, score, neg_large)
        expo = jnp.exp(score - jnp.max(score, axis=0, keepdims=True))
        probs = expo * (1.0 / jnp.sum(expo, axis=0, keepdims=True))
        dprob = dot_nt(values, grad)
        delta = jnp.sum(probs * dprob, axis=0, keepdims=True)
        dscore = (probs * (dprob - delta)).astype(LOW)
        dvalue = dot_nn(probs.astype(LOW), grad)
        dkey = dot_nn(dscore, query)
        dquery = own_heads(dot_tn(dscore, keys), heads)
        query_ref[pl.ds(half_row if near else place, BLOCK), 0:width] = dquery.astype(LOW)
        return dkey, dvalue

    def several(step, carry):
        blk = first + UNROLL * step
        found = [middle(blk + k) for k in range(UNROLL)]
        for k, (dkey, dvalue) in enumerate(found):
            add_rows(key_acc, dkey, blk + k)
            add_rows(value_acc, dvalue, blk + k)
        return carry

    lax.fori_loop(0, count // UNROLL, several, 0)
    for extra in range(count - count % UNROLL, count):
        dkey, dvalue = middle(first + extra)
        add_rows(key_acc, dkey, first + extra)
        add_rows(value_acc, dvalue, first + extra)

    place = walk.place(dense)
    half_row = pl.multiple_of(place - base, BLOCK)
    query = spread_heads(qkv_ref[pl.ds(place, BLOCK), 0:width], heads)
    grad = spread_heads(grad_ref[pl.ds(half_row, BLOCK), :], heads)
    qmark = qmark_ref[pl.ds(dense, 1), :]

    def scores_at(step, top):
        at = pl.multiple_of(step * span, span)
        score = dot_nt(qkv_ref[pl.ds(at, span), width : 2 * width], query)
        score = jnp.where(chunk_marks(mark_ref, walk, at, span) == qmark, score, neg_large)
        score_ref[pl.ds(at, span), :] = score
        dprob_ref[pl.ds(at, span), :] = dot_nt(qkv_ref[pl.ds(at, span), 2 * width : 3 * width], grad)
        return jnp.maximum(top, jnp.max(score, axis=0, keepdims=True))

    def expo_at(step, carry, top):
        total, weighted = carry
        at = pl.multiple_of(step * span, span)
        expo = jnp.exp(score_ref[pl.ds(at, span), :] - top)
        score_ref[pl.ds(at, span), :] = expo
        return (
            total + jnp.sum(expo, axis=0, keepdims=True),
            weighted + jnp.sum(expo * dprob_ref[pl.ds(at, span), :], axis=0, keepdims=True),
        )

    def grads_at(step, dquery, scale, delta):
        at = pl.multiple_of(step * span, span)
        probs = score_ref[pl.ds(at, span), :] * scale
        dscore = (probs * (dprob_ref[pl.ds(at, span), :] - delta)).astype(LOW)
        value_acc[pl.ds(at, span), :] += dot_nn(probs.astype(LOW), grad)
        key_acc[pl.ds(at, span), :] += dot_nn(dscore, query)
        return dquery + dot_tn(dscore, qkv_ref[pl.ds(at, span), width : 2 * width])

    top = jnp.full((1, heads * BLOCK), neg_large, F32)
    top = lax.fori_loop(0, seq // span, scores_at, top)
    total, weighted = lax.fori_loop(0, seq // span, partial(expo_at, top=top), (jnp.zeros_like(top), jnp.zeros_like(top)))
    scale = 1.0 / total
    full = lax.fori_loop(0, seq // span, partial(grads_at, scale=scale, delta=weighted * scale), jnp.zeros((heads * BLOCK, width), F32))
    query_ref[pl.ds(half_row if near else place, BLOCK), 0:width] = own_heads(full, heads).astype(LOW)


def backward_near(rank_ref, pick_ref, qkv_ref, grad_ref, mark_ref, qmark_ref, query_ref, key_acc, value_acc, score_ref, dprob_ref, *, heads, rand, span):
    seq = qkv_ref.shape[0]
    width = heads * HEAD_DIM

    def clear(step, carry):
        at = pl.multiple_of(step * span, span)
        key_acc[pl.ds(at, span), :] = jnp.zeros((span, width), F32)
        value_acc[pl.ds(at, span), :] = jnp.zeros((span, width), F32)
        return carry

    lax.fori_loop(0, seq // span, clear, 0)
    backward_body(rank_ref, pick_ref, qkv_ref, grad_ref, mark_ref, qmark_ref, query_ref, key_acc, value_acc, score_ref, dprob_ref, heads, rand, span, True)


def backward_far(rank_ref, pick_ref, qkv_ref, grad_ref, mark_ref, qmark_ref, near_ref, key_in, value_in, out_ref, key_acc, value_acc, score_ref, dprob_ref, *, heads, rand, span):
    seq = qkv_ref.shape[0]
    width = heads * HEAD_DIM

    def begin(step, carry):
        at = pl.multiple_of(step * span, span)
        key_acc[pl.ds(at, span), :] = key_in[pl.ds(at, span), :]
        value_acc[pl.ds(at, span), :] = value_in[pl.ds(at, span), :]
        return carry

    lax.fori_loop(0, seq // span, begin, 0)
    out_ref[0 : seq // 2, 0:width] = near_ref[...]
    backward_body(rank_ref, pick_ref, qkv_ref, grad_ref, mark_ref, qmark_ref, out_ref, key_acc, value_acc, score_ref, dprob_ref, heads, rand, span, False)

    def finish(step, carry):
        at = pl.multiple_of(step * span, span)
        out_ref[pl.ds(at, span), width : 2 * width] = key_acc[pl.ds(at, span), :].astype(LOW)
        out_ref[pl.ds(at, span), 2 * width : 3 * width] = value_acc[pl.ds(at, span), :].astype(LOW)
        return carry

    lax.fori_loop(0, seq // span, finish, 0)


def token_marks(seq_segs, heads):
    seq = seq_segs.shape[0]
    marks = jnp.where(seq_segs != 0, seq_segs, 1000 + jnp.arange(seq, dtype=jnp.int32))
    by_row = jnp.broadcast_to(marks[:, None], (seq, LANES))
    by_block = jnp.tile(marks.reshape(seq // BLOCK, BLOCK), (1, heads))
    return by_row, by_block


def spent(micros):
    return pl.CostEstimate(flops=micros * 10**9, bytes_accessed=micros * 10**6, transcendentals=0)


SMEM_SPEC = pl.BlockSpec(memory_space=pltpu.SMEM)
VMEM_SPEC = pl.BlockSpec(memory_space=pltpu.VMEM)


def attend(rank, picks, qkv, marks, near):
    heads, _, rand = picks.shape
    seq = qkv.shape[0]
    width = heads * HEAD_DIM
    span = min(512, seq // 4)
    return pl.pallas_call(
        partial(forward_kernel, heads=heads, rand=rand, span=span, near=near),
        out_shape=jax.ShapeDtypeStruct((seq // 2, width), LOW),
        in_specs=[SMEM_SPEC, SMEM_SPEC, VMEM_SPEC, VMEM_SPEC, VMEM_SPEC],
        out_specs=VMEM_SPEC,
        scratch_shapes=[pltpu.VMEM((seq, heads * BLOCK), F32)],
        name="attend_near" if near else "attend_far",
        cost_estimate=spent(1),
    )(rank, picks.reshape(-1), qkv, *marks)


def attend_back_near(rank, picks, qkv, grad_context, marks):
    heads, _, rand = picks.shape
    seq = qkv.shape[0]
    width = heads * HEAD_DIM
    span = min(512, seq // 4)
    total = jax.ShapeDtypeStruct((seq, width), F32)
    return pl.pallas_call(
        partial(backward_near, heads=heads, rand=rand, span=span),
        out_shape=[jax.ShapeDtypeStruct((seq // 2, width), LOW), total, total],
        in_specs=[SMEM_SPEC, SMEM_SPEC, VMEM_SPEC, VMEM_SPEC, VMEM_SPEC, VMEM_SPEC],
        out_specs=[VMEM_SPEC] * 3,
        scratch_shapes=[pltpu.VMEM((seq, heads * BLOCK), F32)] * 2,
        name="attend_back_near",
        cost_estimate=spent(40),
    )(rank, picks.reshape(-1), qkv, grad_context, *marks)


def attend_back_far(rank, picks, qkv, grad_context, marks, near_parts):
    heads, _, rand = picks.shape
    seq = qkv.shape[0]
    width = heads * HEAD_DIM
    span = min(512, seq // 4)
    return pl.pallas_call(
        partial(backward_far, heads=heads, rand=rand, span=span),
        out_shape=jax.ShapeDtypeStruct((seq, 3 * width), LOW),
        in_specs=[SMEM_SPEC, SMEM_SPEC] + [VMEM_SPEC] * 7,
        out_specs=VMEM_SPEC,
        scratch_shapes=[pltpu.VMEM((seq, width), F32)] * 2 + [pltpu.VMEM((seq, heads * BLOCK), F32)] * 2,
        name="attend_back_far",
        cost_estimate=spent(43),
    )(rank, picks.reshape(-1), qkv, grad_context, *marks, *near_parts)


eps_norm = 1e-05


def by_rows(values):
    return with_layout_constraint(values, Layout(major_to_minor=(0, 1)))


def tie(values, *others):
    return lax.optimization_barrier((values, others))[0]


def norm_rows(source, gain_vec, shift_vec):
    average = jnp.mean(source, axis=-1, keepdims=True)
    centred = source - average
    variance = jnp.mean(centred * centred, axis=-1, keepdims=True)
    return centred * lax.rsqrt(variance + eps_norm) * gain_vec + shift_vec


def norm_kernel(source_ref, gain_ref, shift_ref, out_ref):
    step = min(128, source_ref.shape[0])

    def turn(index, carry):
        rows = pl.ds(pl.multiple_of(index * step, step), step)
        out_ref[rows, :] = norm_rows(source_ref[rows, :].astype(F32), gain_ref[...], shift_ref[...]).astype(LOW)
        return carry

    lax.fori_loop(0, source_ref.shape[0] // step, turn, 0)


def norm_call(source, gain, shift):
    rows, model = source.shape
    tile = min(512, rows)
    vector = pl.BlockSpec((1, model), lambda i: (0, 0))
    block = pl.BlockSpec((tile, model), lambda i: (i, 0))
    return pl.pallas_call(
        norm_kernel,
        grid=(rows // tile,),
        in_specs=[block, vector, vector],
        out_specs=block,
        out_shape=jax.ShapeDtypeStruct((rows, model), LOW),
        name="norm",
        cost_estimate=spent(3),
    )(source, gain, shift)


def norm_back_kernel(source_ref, gain_ref, residual_ref, *rest, terms, narrow):
    term_refs = rest[:terms]
    out_ref = rest[terms]
    low_ref = rest[terms + 1] if narrow else None
    sum_ref = rest[-1]
    model = source_ref.shape[1]
    step = min(128, source_ref.shape[0])

    def turn(index, parts):
        rows = pl.ds(pl.multiple_of(index * step, step), step)
        source = source_ref[rows, :].astype(F32)
        grad = term_refs[0][rows, :].astype(F32)
        for ref in term_refs[1:]:
            grad = grad + ref[rows, :].astype(F32)
        centred = source - jnp.mean(source, axis=-1, keepdims=True)
        scale = lax.rsqrt(jnp.mean(centred * centred, axis=-1, keepdims=True) + eps_norm)
        normal = centred * scale
        scaled = grad * gain_ref[...]
        first = jnp.mean(scaled, axis=-1, keepdims=True)
        second = jnp.mean(scaled * normal, axis=-1, keepdims=True)
        residual = residual_ref[rows, :].astype(F32)
        full = residual + scale * (scaled - first - normal * second)
        out_ref[rows, :] = full
        if narrow:
            low_ref[rows, :] = full.astype(LOW)
        found = [grad * normal, grad] + ([residual] if narrow else [])
        return tuple(part + jnp.sum(term, axis=0, keepdims=True) for part, term in zip(parts, found))

    parts = tuple(jnp.zeros((1, model), F32) for _ in range(2 + narrow))
    parts = lax.fori_loop(0, source_ref.shape[0] // step, turn, parts)
    parts = jnp.concatenate(parts + (jnp.zeros((8 - len(parts), model), F32),), axis=0)

    @pl.when(pl.program_id(0) == 0)
    def _():
        sum_ref[...] = parts

    @pl.when(pl.program_id(0) != 0)
    def _():
        sum_ref[...] += parts


def norm_back(source, gain, residual, terms, narrow):
    rows, model = source.shape
    tile = min(512, rows)
    vector = pl.BlockSpec((1, model), lambda i: (0, 0))
    block = pl.BlockSpec((tile, model), lambda i: (i, 0))
    shapes = [jax.ShapeDtypeStruct((rows, model), F32)]
    if narrow:
        shapes.append(jax.ShapeDtypeStruct((rows, model), LOW))
    return pl.pallas_call(
        partial(norm_back_kernel, terms=len(terms), narrow=narrow),
        grid=(rows // tile,),
        in_specs=[block, vector] + [block] * (1 + len(terms)),
        out_specs=[block] * len(shapes) + [pl.BlockSpec((8, model), lambda i: (0, 0))],
        out_shape=shapes + [jax.ShapeDtypeStruct((8, model), F32)],
        name="norm_back",
        cost_estimate=spent(7),
    )(source, gain, residual, *terms)


def down_kernel(hidden_ref, part_ref, down_ref, side_ref, own_ref, *, step):
    def run(out_ref):
        def turn(index, carry):
            rows = pl.ds(pl.multiple_of(index * step, step), step)
            out_ref[rows, :] = (part_ref[rows, :] + dot_nt(hidden_ref[rows, :], down_ref[...])).astype(out_ref.dtype)
            return carry

        lax.fori_loop(0, hidden_ref.shape[0] // step, turn, 0)

    @pl.when(pl.program_id(0) == 0)
    def _():
        run(side_ref)

    @pl.when(pl.program_id(0) == 1)
    def _():
        run(own_ref)


def down_call(hidden, part, weights):
    rows = hidden.shape[0] // 2
    units = hidden.shape[1]
    model = weights.shape[0]
    last = weights.shape[1] // units - 1
    out = pl.BlockSpec((rows, model), lambda t: (0, 0))
    return pl.pallas_call(
        partial(down_kernel, step=min(256, rows)),
        grid=(2,),
        in_specs=[
            pl.BlockSpec((rows, units), lambda t: (1 - t, 0)),
            pl.BlockSpec((rows, model), lambda t: (1 - t, 0)),
            pl.BlockSpec((model, units), lambda t: (0, last)),
        ],
        out_specs=[out, out],
        out_shape=[jax.ShapeDtypeStruct((rows, model), LOW), jax.ShapeDtypeStruct((rows, model), F32)],
        name="down",
        cost_estimate=spent(1),
    )(hidden, part, weights)


def finish_kernel(middle_ref, own_ref, back_ref, bias_ref, valid_ref, out_ref, sum_ref):
    branch = own_ref[...] + back_ref[...].astype(F32) + bias_ref[...]
    out_ref[...] = (middle_ref[...] + branch).astype(LOW)
    squares = jnp.sum(valid_ref[...] * branch * branch, axis=0, keepdims=True)

    @pl.when(pl.program_id(0) == 0)
    def _():
        sum_ref[...] = squares

    @pl.when(pl.program_id(0) != 0)
    def _():
        sum_ref[...] += squares


def finish_call(middle, own, back, bias, valid):
    rows, model = middle.shape
    tile = min(512, rows)
    vector = pl.BlockSpec((1, model), lambda i: (0, 0))
    block = pl.BlockSpec((tile, model), lambda i: (i, 0))
    return pl.pallas_call(
        finish_kernel,
        grid=(rows // tile,),
        in_specs=[block, block, block, vector, pl.BlockSpec((tile, 1), lambda i: (i, 0))],
        out_specs=[block, vector],
        out_shape=[jax.ShapeDtypeStruct((rows, model), LOW), jax.ShapeDtypeStruct((1, model), F32)],
        name="finish",
        cost_estimate=spent(1),
    )(middle, own, back, bias, valid)


def feed_kernel(second_own, second_side, grad_own, grad_side, up_ref, down_ref, bias_ref, hidden_ref, pre_ref, sum_ref, *, step):
    slope = (2.0 / jnp.pi) ** 0.5

    def run(second_ref, grad_ref):
        def chunk(at):
            rows = pl.ds(pl.multiple_of(at, step), step)
            unit = dot_nn(second_ref[rows, :], up_ref[...]) + bias_ref[...]
            grad = dot_nn(grad_ref[rows, :], down_ref[...])
            square = unit * unit
            bent = jnp.tanh(unit * (slope + (slope * 0.044715) * square))
            half = 0.5 + 0.5 * bent
            hidden_ref[rows, :] = (unit * half).astype(LOW)
            rise = half + (0.5 * unit) * (1.0 - bent * bent) * (slope + (slope * 0.134145) * square)
            low = (grad * rise).astype(LOW)
            pre_ref[rows, :] = low
            return jnp.sum(low.astype(F32), axis=0, keepdims=True)

        def turn(index, total):
            return total + chunk(2 * step * index) + chunk(2 * step * index + step)

        sum_ref[0] = lax.fori_loop(0, second_ref.shape[0] // (2 * step), turn, jnp.zeros(sum_ref.shape[1:], F32))

    @pl.when(pl.program_id(0) == 0)
    def _():
        run(second_own, grad_own)

    @pl.when(pl.program_id(0) == 1)
    def _():
        run(second_side, grad_side)


def feed(seconds, grads, weights, first_up, first_down, bias):
    rows, model = seconds[0].shape
    units = bias.shape[0]
    tile = min(512, units)
    whole = pl.BlockSpec((rows, model), lambda t, u: (0, 0))
    out = pl.BlockSpec((rows, tile), lambda t, u: (t, u))
    return pl.pallas_call(
        partial(feed_kernel, step=min(128, rows)),
        grid=(2, units // tile),
        in_specs=[whole] * 4
        + [
            pl.BlockSpec((model, tile), lambda t, u: (0, first_up // tile + u)),
            pl.BlockSpec((model, tile), lambda t, u: (0, first_down // tile + u)),
            pl.BlockSpec((1, tile), lambda t, u: (0, u)),
        ],
        out_specs=[out, out, pl.BlockSpec((1, 1, tile), lambda t, u: (t, 0, u))],
        out_shape=[
            jax.ShapeDtypeStruct((2 * rows, units), LOW),
            jax.ShapeDtypeStruct((2 * rows, units), LOW),
            jax.ShapeDtypeStruct((2, 1, units), F32),
        ],
        name="feed",
        cost_estimate=spent(3),
    )(*seconds, *grads, weights, weights, bias[None])


def swap(values, axis, mask):
    count = lax.axis_size(axis)
    return lax.ppermute(values, axis, [(i, i ^ mask) for i in range(count)])


def collect_rows(parts, *hooks):
    hooks = list(hooks)
    count = lax.axis_size("fsdp")
    spot = lax.axis_index("fsdp")
    rows = parts[0].shape[0] // count
    mask = 1
    while mask < count:
        upper = (spot & mask) != 0
        parts = [part.reshape(-1, 2, rows, part.shape[-1]) for part in parts]
        sent = [jnp.where(upper, part[:, 0], part[:, 1]).astype(LOW) for part in parts]
        got = swap(jnp.concatenate(sent, -1), "fsdp", mask)
        first = 0
        held = []
        for part in parts:
            last = first + part.shape[-1]
            held.append(jnp.where(upper, part[:, 1], part[:, 0]) + got[..., first:last].astype(F32))
            first = last
        parts = hooks.pop(0)(held) if hooks else held
        mask *= 2
    return [part.reshape(rows, part.shape[-1]) for part in parts]


def total_over(values, axis):
    bits = [1 << k for k in range(lax.axis_size(axis).bit_length() - 1)]
    while bits:
        if len(bits) % 2:
            values = values + swap(values, axis, bits.pop(0))
        else:
            low, high = bits.pop(0), bits.pop(0)
            values = (values + swap(values, axis, low)) + (swap(values, axis, high) + swap(values, axis, low | high))
    return values


def on_device(
    hidden_in,
    cotangent,
    norm1_gain,
    norm1_bias,
    w_query,
    w_key,
    w_value,
    w_out,
    norm2_gain,
    norm2_bias,
    w_fc1,
    bias_fc1,
    w_fc2,
    bias_fc2,
    segments,
    random_blocks,
):
    rows_dev, width_model = hidden_in.shape
    heads_wide = w_query.shape[1]
    rank = lax.axis_index("tp")
    seq_segs = segments[0]
    picks = random_blocks[0]
    heads_local = picks.shape[0]
    own_segs = lax.dynamic_slice_in_dim(seq_segs, rank * rows_dev, rows_dev)
    valid_rows = (own_segs != 0).astype(F32)[:, None]
    gain_first = norm1_gain.astype(F32)[None]
    shift_first = norm1_bias.astype(F32)[None]
    gain_second = norm2_gain.astype(F32)[None]
    shift_second = norm2_bias.astype(F32)[None]
    residual_in = hidden_in.astype(F32)
    scale_query = HEAD_DIM ** (-0.5)
    rank_word = rank.astype(jnp.int32).reshape(1)
    marks = token_marks(seq_segs, heads_local)

    heads_local_w = by_rows(jnp.concatenate([w_query * jnp.asarray(scale_query, LOW), w_key, w_value, w_out.T], 1))
    w_heads = lax.all_gather(heads_local_w, "fsdp", axis=0, tiled=True)
    pair_local = by_rows(jnp.concatenate([w_fc1, w_fc2.T], 1))
    units = w_fc1.shape[1]
    own_all = lax.all_gather(pair_local, "fsdp", axis=0, tiled=True)
    far_hidden = swap(hidden_in, "tp", 2)
    far_local = swap(tie(pair_local, far_hidden), "tp", 2)
    bias_up = [bias_fc1.astype(F32), swap(bias_fc1, "tp", 2).astype(F32)]

    first_own = norm_call(tie(hidden_in, marks, picks), gain_first, shift_first)
    first_side = swap(first_own, "tp", 1)
    far_hidden, w_heads = lax.optimization_barrier((far_hidden, w_heads))
    w_qkv = w_heads[:, : 3 * heads_wide]
    first_far = norm_call(far_hidden, gain_first, shift_first)
    first_cross = swap(first_far, "tp", 1)
    chunks = (first_own, first_side, first_far, first_cross)
    qkv = jnp.concatenate([dot_nn(chunk, w_qkv).astype(LOW) for chunk in chunks], 0)
    qkv, far_local = lax.optimization_barrier((qkv, far_local))
    far_all = lax.all_gather(far_local, "fsdp", axis=0, tiled=True)
    context_far = attend(rank_word, picks, qkv, marks, False)
    context_cross = [swap(context_far[k * rows_dev : (k + 1) * rows_dev], "tp", 2 + k) for k in (0, 1)]
    wo_own = tie(w_heads, qkv)[:, 3 * heads_wide :]
    wo_pair = jnp.concatenate([wo_own, swap(wo_own, "tp", 2)], 1)
    wo_side = swap(wo_pair, "tp", 1)
    wo_all = by_rows(jnp.concatenate(
        [wo_pair[:, :heads_wide], wo_side[:, :heads_wide], wo_pair[:, heads_wide:], wo_side[:, heads_wide:]], 1
    ))
    context_near = attend(rank_word, picks, tie(qkv, context_far), marks, True)
    side_context, context_cross = lax.optimization_barrier((context_near[rows_dev:], context_cross))
    context_cat = by_rows(jnp.concatenate(
        [context_near[:rows_dev], swap(side_context, "tp", 1)] + context_cross, 1
    ))
    attn_branch = by_rows(dot_nt(context_cat, wo_all))
    middle = residual_in + attn_branch
    early_rows = jnp.concatenate(
        [jnp.full((1, width_model), jnp.sum(valid_rows))]
        + [
            jnp.sum(valid_rows * branch * branch, axis=0, keepdims=True)
            for branch in (residual_in, attn_branch, middle)
        ]
    )
    second_own = by_rows(norm_rows(middle, gain_second, shift_second).astype(LOW))

    second_side = swap(second_own, "tp", 1)
    grad_side = swap(cotangent, "tp", 1)
    tokens = (second_own, second_side), (cotangent, grad_side)
    first = feed(*tokens, own_all, 0, units, bias_up[0])
    down_part = by_rows(dot_nt(first[0], own_all[:, units:]))
    up_part = by_rows(dot_nt(first[1], own_all[:, :units]))
    far_all, down_part, up_part = lax.optimization_barrier((far_all, down_part, up_part))
    hidden, grad_pre, bias_parts = zip(first, feed(*tokens, far_all, 0, units, bias_up[1]))
    w_up_far = far_all[:, :units]
    side_terms = up_part[rows_dev:] + dot_nt(grad_pre[1][rows_dev:], w_up_far)
    side_back = swap(by_rows(side_terms.astype(LOW)), "tp", 1)
    own_terms = up_part[:rows_dev] + dot_nt(grad_pre[1][:rows_dev], w_up_far)
    second_two = jnp.concatenate([second_own, second_side], 0)
    grad_two = jnp.concatenate([cotangent, grad_side], 0)
    share = by_rows(jnp.concatenate(
        [dot_tn(second_two, grad_pre[half]).astype(LOW) for half in range(2)]
        + [dot_tn(grad_two, hidden[half]).astype(LOW) for half in range(2)],
        1,
    ))
    grad_middle, grad_attn, second_sums = norm_back(middle, gain_second, cotangent, (by_rows(own_terms), side_back), True)

    grad_context_cat = dot_nn(grad_attn, wo_all).astype(LOW)
    grad_parts = [grad_context_cat[:, k * heads_wide : (k + 1) * heads_wide] for k in range(4)]
    grad_far = jnp.concatenate([swap(grad_parts[2], "tp", 2), swap(grad_parts[3], "tp", 3)], 0)
    grad_near = jnp.concatenate([grad_parts[0], swap(grad_parts[1], "tp", 1)], 0)
    out_terms = by_rows(dot_tn(grad_attn, context_cat))
    out_near = [out_terms[:, k * heads_wide : (k + 1) * heads_wide] for k in range(4)]
    out_chip = [
        out_near[k] + swap(out_near[k + 1].astype(LOW), "tp", 1).astype(F32) for k in (0, 2)
    ]
    out_sum = out_chip[0] + swap(out_chip[1].astype(LOW), "tp", 2).astype(F32)
    grad_near, share, out_terms = lax.optimization_barrier((grad_near, share, out_terms))
    share = lax.psum_scatter(share, "fsdp", scatter_dimension=0, tiled=True)
    near_parts = attend_back_near(rank_word, picks, qkv, grad_near, marks)
    bias_terms = [jnp.sum(parts, axis=0) for parts in bias_parts]
    grad_bias_up = bias_terms[0] + swap(bias_terms[1], "tp", 2)
    out_sum, grad_far, near_parts, grad_bias_up = lax.optimization_barrier(
        (out_sum, grad_far, near_parts, grad_bias_up)
    )
    grad_qkv = attend_back_far(rank_word, picks, qkv, grad_far, marks, near_parts)
    far_side = by_rows(dot_nt(grad_qkv[3 * rows_dev :], w_qkv).astype(LOW))
    far_own = by_rows(dot_nt(grad_qkv[2 * rows_dev : 3 * rows_dev], w_qkv))
    far_side, far_own = lax.optimization_barrier((swap(far_side, "tp", 1), far_own))
    far_low = (far_own + far_side.astype(F32)).astype(LOW)
    far_back = swap(far_low, "tp", 2)

    grad_qkv_late = tie(grad_qkv, far_low)
    qkv_terms = by_rows(dot_tn(jnp.concatenate(chunks, 0), grad_qkv_late))
    hidden_far, grad_qkv_late = tie((hidden[1], grad_qkv_late), qkv_terms)
    near_side = by_rows(dot_nt(grad_qkv_late[rows_dev : 2 * rows_dev], w_qkv).astype(LOW))
    near_own = by_rows(dot_nt(grad_qkv_late[:rows_dev], w_qkv))
    near_back = swap(near_side, "tp", 1)
    down_side, down_own = down_call(hidden_far, down_part, far_all)
    output_rows, branch_squares = finish_call(
        middle, down_own, swap(down_side, "tp", 1), bias_fc2.astype(F32)[None], valid_rows
    )
    square_rows = jnp.concatenate([early_rows, branch_squares])

    gathered = {}

    def after_first(parts):
        parts, (back, rows_out, squares, part, near) = lax.optimization_barrier(
            (parts, (far_back, output_rows, square_rows, share, near_back))
        )
        part = part.astype(F32)
        cross = jnp.concatenate([part[:, units : 2 * units], part[:, 3 * units :]], 1)
        cross = swap(cross.astype(LOW), "tp", 2)
        grad_in, sums_in = norm_back(hidden_in, gain_first, grad_middle, (near_own, near, back), False)
        gathered.update(share=part, across=cross, output=rows_out, squares=squares, input=grad_in, sums=sums_in)
        return parts

    def after_second(parts):
        parts, gathered["sums"], gathered["across"] = lax.optimization_barrier(
            (parts, gathered["sums"], gathered["across"])
        )
        return parts

    collected, grad_w_o = collect_rows([qkv_terms, out_sum], after_first, after_second)
    share, across, first_sums = gathered["share"], gathered["across"], gathered["sums"]
    output_rows, square_rows, grad_input = gathered["output"], gathered["squares"], gathered["input"]
    across = across.astype(F32)
    grad_w_up = share[:, :units] + across[:, :units]
    grad_w_down = (share[:, 2 * units : 3 * units] + across[:, units:]).T
    grad_w_q = collected[:, :heads_wide] * scale_query
    grad_w_k = collected[:, heads_wide : 2 * heads_wide]
    grad_w_v = collected[:, 2 * heads_wide :]
    grad_w_o = grad_w_o.T

    sums = jnp.concatenate([second_sums[:3], square_rows, first_sums[:2]])
    sums = total_over(sums, "tp")
    bias_rows = grad_bias_up.reshape(-1, width_model)
    sums = total_over(jnp.concatenate([sums, bias_rows]), "fsdp")
    residual_rms = jnp.sqrt(jnp.sum(sums[4:8], axis=1) / (sums[3, 0] * width_model))
    return (
        output_rows,
        grad_input,
        sums[8],
        sums[9],
        grad_w_q,
        grad_w_k,
        grad_w_v,
        grad_w_o,
        sums[0],
        sums[1],
        grad_w_up,
        sums[10:].reshape(-1),
        grad_w_down,
        sums[2],
        residual_rms,
    )


def solution(mesh):
    in_specs = (
        P(("fsdp", "tp"), None),
        P(("fsdp", "tp"), None),
        P(),
        P(),
        P("fsdp", "tp"),
        P("fsdp", "tp"),
        P("fsdp", "tp"),
        P("tp", "fsdp"),
        P(),
        P(),
        P("fsdp", "tp"),
        P("tp"),
        P("tp", "fsdp"),
        P(),
        P("fsdp", None),
        P("fsdp", "tp", None, None),
    )
    out_specs = (
        P(("fsdp", "tp"), None),
        P(("fsdp", "tp"), None),
        P(),
        P(),
        P("fsdp", "tp"),
        P("fsdp", "tp"),
        P("fsdp", "tp"),
        P("tp", "fsdp"),
        P(),
        P(),
        P("fsdp", "tp"),
        P("tp"),
        P("tp", "fsdp"),
        P(),
        P(),
    )
    return jax.shard_map(
        on_device, mesh=mesh, in_specs=in_specs, out_specs=out_specs, check_vma=False
    )
```
